128 devices in a mesh: cfg: 2 (over core), seq: 64 (over z, y, x).
Axes of the slice: x: 4, y: 4, z: 4, core: 2. Of those that a mesh axis runs over, the one named last changes fastest.
Arguments:
- hidden: bfloat16 [2, 512, 3072], P('cfg', 'seq'), may hold values from -6 to 6
- latent: float32 [512, 64], P('seq', 'cfg'), may hold values from -6 to 6
- positions: int32 [512, 3], P('seq'), may hold values from 0 to 44
- counts: int32 [64], replicated, may hold values from 4 to 8
- text_len: int32 [1], replicated, may hold values from 1 to 255
- modulation: float32 [2, 6, 3072], replicated, may hold values from -3 to 3
- w_qkv: bfloat16 [3072, 3, 3072], P(None, None, 'seq'), may hold values from -0.109375 to 0.109375
- w_out: bfloat16 [3072, 3072], P('seq'), may hold values from -0.109375 to 0.109375
- w_up: bfloat16 [3072, 12288], P(None, 'seq'), may hold values from -0.109375 to 0.109375
- w_down: bfloat16 [12288, 3072], P('seq'), may hold values from -0.0546875 to 0.0546875
- out_mod: float32 [2, 3072], replicated, may hold values from -3 to 3
- w_proj: bfloat16 [3072, 64], replicated, may hold values from -0.109375 to 0.109375
- guidance: float32 [1], replicated, may hold values from 3 to 8
- solver: float32 [2], replicated, may hold values from 0.3 to 1
Outputs:
- next_latent: float32 [512, 64], P('seq', 'cfg')
The draws below stay inside these ranges and needn't reach their ends.
All inputs are finite; a program needn't handle non-finite values.
Results may differ from the reference program's by a relative error of at most 0.009.
Values may be sent and summed in bfloat16 or wider, within the bound.
A program may use at most 128 MiB of HBM per device.

```python
import jax
import jax.numpy as jnp
from jax import lax

D = 3072
HD = 64
FF = 12288
P_SIZE = 64
TOK_DEV = 8
SEQ = 512
N_SEQ = 64


def touch_ends(drawn, key, least, top_value):
    spot = [jax.random.randint(jax.random.fold_in(key, axis), (), 0, length) for axis, length in enumerate(drawn.shape)]
    longest = drawn.shape.index(max(drawn.shape))
    next_to = spot[:longest] + [(spot[longest] + 1) % drawn.shape[longest]] + spot[longest + 1:]
    return drawn.at[tuple(spot)].set(least).at[tuple(next_to)].set(top_value)


def block_levels(key, extent, cuts, smallest, largest):
    def one(dim, shards_of):
        draws = jax.random.uniform(jax.random.fold_in(jax.random.fold_in(key, 6), dim), (shards_of,), jnp.float32, smallest / len(cuts), largest / len(cuts))
        return jnp.repeat(jnp.exp(draws), extent[dim] // shards_of).reshape((-1,) + (1,) * (len(extent) - dim - 1))

    loudness = one(*cuts[0])
    for cut in cuts[1:]:
        loudness = loudness * one(*cut)
    return loudness


def bell_draw(key, extent, scale, limit, pieces=(), held_as=jnp.bfloat16):
    drawn = jax.random.normal(key, extent, jnp.float32) * scale
    if len(pieces) > 0:
        drawn = block_levels(key, extent, pieces, -0.22, 0.18) * drawn
    return jnp.clip(drawn, min=-limit, max=limit).astype(held_as)


def setup_inputs(seed: int = 0) -> dict:
    key_list = jax.random.split(jax.random.key(seed), 15)
    return {
        "hidden": bell_draw(key_list[0], (2, SEQ, D), 1.0, 6.0, ((0, 2), (1, 64))),
        "latent": bell_draw(key_list[1], (SEQ, P_SIZE), 1.0, 6.0, ((0, 64), (1, 2)), jnp.float32),
        "positions": touch_ends(jax.random.randint(key_list[2], (SEQ, 3), 0, 45), jax.random.fold_in(key_list[2], 1), 0, 44).astype(jnp.int32),
        "counts": touch_ends(jax.random.randint(key_list[3], (N_SEQ,), TOK_DEV // 2, TOK_DEV + 1), jax.random.fold_in(key_list[3], 1), TOK_DEV // 2, TOK_DEV).astype(jnp.int32),
        "text_len": jax.random.randint(key_list[4], (1,), 1, SEQ // 2).astype(jnp.int32),
        "modulation": bell_draw(key_list[5], (2, 6, D), 0.5, 3.0, (), jnp.float32),
        "w_qkv": bell_draw(key_list[6], (D, 3, D), D ** -0.5, 0.109375, ((2, 64),)),
        "w_out": bell_draw(key_list[7], (D, D), D ** -0.5, 0.109375, ((0, 64),)),
        "w_up": bell_draw(key_list[8], (D, FF), D ** -0.5, 0.109375, ((1, 64),)),
        "w_down": bell_draw(key_list[9], (FF, D), FF ** -0.5, 0.0546875, ((0, 64),)),
        "out_mod": bell_draw(key_list[10], (2, D), 0.5, 3.0, (), jnp.float32),
        "w_proj": bell_draw(key_list[11], (D, P_SIZE), D ** -0.5, 0.109375),
        "guidance": jnp.clip(jax.random.uniform(key_list[12], (1,), jnp.float32, 3.0, 8.0), 3.0, 8.0),
        "solver": jnp.clip(jax.random.uniform(key_list[13], (2,), jnp.float32, 0.3, 1.0), 0.3, 1.0),
    }


def layer_norm(values, epsilon):
    center = values - lax.optimization_barrier(jnp.mean(values, axis=-1, keepdims=True))
    spread = lax.optimization_barrier(jnp.mean(center * center, axis=-1, keepdims=True))
    return center * lax.rsqrt(spread + epsilon)

def rotary_angles(position_rows, head_size):
    places = position_rows.astype(jnp.float32)
    frame_pairs = head_size // 8
    side_pairs = 3 * head_size // 16
    frame_freq = 10000.0 ** (-2.0 * jnp.arange(frame_pairs, dtype=jnp.float32) / (head_size // 4))
    side_freq = 10000.0 ** (-2.0 * jnp.arange(side_pairs, dtype=jnp.float32) / (3 * head_size // 8))
    return jnp.concatenate([places[:, 0:1] * frame_freq[None, :], places[:, 1:2] * side_freq[None, :], places[:, 2:3] * side_freq[None, :]], axis=1)

def prepare_heads(columns, cosine, sine, heads, head_size):
    values = columns.astype(jnp.float32).reshape(columns.shape[0], heads, head_size)
    values = layer_norm(values, 1e-06)
    pairs = values.reshape(columns.shape[0], heads, head_size // 2, 2)
    first = pairs[..., 0]
    second = pairs[..., 1]
    cos_rows = cosine[:, None, :]
    sin_rows = sine[:, None, :]
    turned = jnp.stack([first * cos_rows - second * sin_rows, first * sin_rows + second * cos_rows], axis=-1)
    return turned.reshape(columns.shape[0], heads * head_size).astype(jnp.bfloat16)

def reference(hidden, latent, positions, counts, text_len, modulation, w_qkv, w_out, w_up, w_down, out_mod, w_proj, guidance, solver):
    heads = D // HD
    slots = jnp.arange(SEQ)
    live = slots % TOK_DEV < jnp.repeat(counts, TOK_DEV)
    is_text = slots < text_len[0]
    angles = rotary_angles(positions, HD) * jnp.where(is_text, 0.0, 1.0)[:, None].astype(jnp.float32)
    cosine = jnp.cos(angles)
    sine = jnp.sin(angles)
    live_weight = jnp.where(live, 1.0, 0.0).astype(jnp.float32)

    def modul(index):
        return jnp.where(is_text[:, None], modulation[0, index][None, :], modulation[1, index][None, :])

    def branch(tokens):
        resid = tokens.astype(jnp.float32)
        normed = (layer_norm(resid, 1e-05) * (1.0 + modul(1)) + modul(0)).astype(jnp.bfloat16)
        qkv = jnp.dot(normed, w_qkv.reshape(D, 3 * D), preferred_element_type=jnp.float32).astype(jnp.bfloat16)
        qkv = qkv.reshape(SEQ, 3, D)
        queries = prepare_heads(qkv[:, 0], cosine, sine, heads, HD)
        keys_rot = prepare_heads(qkv[:, 1], cosine, sine, heads, HD)
        values = qkv[:, 2]
        q_heads = jnp.swapaxes(queries.reshape(SEQ, heads, HD), 0, 1)
        k_heads = jnp.swapaxes(keys_rot.reshape(SEQ, heads, HD), 0, 1)
        v_heads = jnp.swapaxes(values.reshape(SEQ, heads, HD), 0, 1)

        def one_head(operands):
            q_one, k_one, v_one = operands
            scores = jnp.dot(q_one, k_one.T, preferred_element_type=jnp.float32) * HD ** (-0.5)
            weights = jnp.exp(scores) * live_weight[None, :]
            denom = lax.optimization_barrier(jnp.sum(weights, axis=1))
            numer = jnp.dot(weights.astype(jnp.bfloat16), v_one, preferred_element_type=jnp.float32)
            return (numer / denom[:, None]).astype(jnp.bfloat16)
        context = lax.map(one_head, (q_heads, k_heads, v_heads))
        context = jnp.swapaxes(context, 0, 1).reshape(SEQ, D)
        attended = jnp.dot(context, w_out, preferred_element_type=jnp.float32)
        first_res = resid + modul(2) * attended
        normed_two = (layer_norm(first_res, 1e-05) * (1.0 + modul(4)) + modul(3)).astype(jnp.bfloat16)
        inner = jax.nn.gelu(jnp.dot(normed_two, w_up, preferred_element_type=jnp.float32), approximate=True).astype(jnp.bfloat16)
        second_res = first_res + modul(5) * jnp.dot(inner, w_down, preferred_element_type=jnp.float32)
        final = (layer_norm(second_res, 1e-05) * (1.0 + out_mod[1][None, :]) + out_mod[0][None, :]).astype(jnp.bfloat16)
        return jnp.dot(final, w_proj, preferred_element_type=jnp.float32)
    pred_cond = branch(hidden[0])
    pred_uncond = branch(hidden[1])
    guided = pred_uncond + guidance[0] * (pred_cond - pred_uncond)
    updated = solver[0] * latent + solver[1] * guided
    return jnp.where((live & jnp.logical_not(is_text))[:, None], updated, latent)
```

```python
import functools

import jax
import jax.numpy as jnp
import numpy as np
from jax import lax
from jax.experimental import pallas as pl
from jax.experimental.pallas import tpu as pltpu
from jax.sharding import PartitionSpec as P

D = 3072
HD = 64
SIDE = 4
ROWS = 8
HALF = D // 2
HC = 192
HID = 192
PAD = 128
BF = jnp.bfloat16
F32 = jnp.float32
NT = (((1,), (1,)), ((), ()))


def layer_norm(values, epsilon):
    center = values - jnp.mean(values, axis=-1, keepdims=True)
    spread = jnp.mean(center * center, axis=-1, keepdims=True)
    return center * lax.rsqrt(spread + epsilon)


def dot_nt(a, b):
    return lax.dot_general(a, b, NT, preferred_element_type=F32)


def exact_dot(a, b):
    return lax.dot_general(
        a,
        b,
        (((1,), (0,)), ((), ())),
        preferred_element_type=F32,
        precision=lax.Precision.HIGHEST,
    )


def frequencies():
    frame = 10000.0 ** (-2.0 * np.arange(8) / 16)
    side = 10000.0 ** (-2.0 * np.arange(12) / 24)
    pairs = np.concatenate([frame, side, side])
    return np.tile(np.repeat(pairs, 2), 3)[None, :].astype(np.float32)


def kernel(
    hidden,
    latent,
    pos,
    counts_row,
    counts,
    text_len,
    modulation,
    freq,
    w_qkv,
    w_out,
    w_up,
    w_down,
    out_mod,
    w_proj,
    guidance,
    solver,
    out,
    wqkv,
    wout,
    wup,
    wdown,
    ag1a,
    ag1b,
    ag2a,
    ag2b,
    rows32,
    kv,
    rs1,
    rs2,
    swap,
    w_send,
    w_recv,
    f_send,
    f_recv,
    local_sem,
    c_send,
    c_recv,
):
    cfg = lax.axis_index("cfg")
    me = lax.axis_index("seq")
    z, y, x = me // 16, (me // 4) % 4, me % 4

    def dev(axis, step):
        zz = (z + step) % 4 if axis == "z" else z
        yy = (y + step) % 4 if axis == "y" else y
        xx = (x + step) % 4 if axis == "x" else x
        return (cfg, zz * 16 + yy * 4 + xx)

    place = {"x": x, "y": y, "z": z}
    sibling = (1 - cfg, me)
    sends = []

    def remote(src, dst, send, recv, device):
        copy = pltpu.make_async_remote_copy(
            src_ref=src,
            dst_ref=dst,
            send_sem=send,
            recv_sem=recv,
            device_id=device,
            device_id_type=pl.DeviceIdType.MESH,
        )
        copy.start()
        sends.append(copy)
        return copy

    barrier = pltpu.get_barrier_semaphore()
    everyone = [dev(axis, step) for axis in "xyz" for step in (1, 2, 3)] + [sibling]
    for device in everyone:
        pl.semaphore_signal(
            barrier, inc=1, device_id=device, device_id_type=pl.DeviceIdType.MESH
        )

    mine = pl.ds(pl.multiple_of(cfg * HALF, HALF), HALF)

    weights = {
        "qkv": (0, w_qkv, lambda i: wqkv.at[:, i], "x"),
        "out": (1, w_out, lambda i: wout.at[i], "x"),
        "up": (2, w_up, lambda i: wup.at[i], "y"),
        "down": (3, w_down, lambda i: wdown.at[i], "y"),
    }

    def half_of(ref):
        return ref.at[:, :, mine] if len(ref.shape) == 3 else ref.at[:, mine]

    pending = {}

    def start_weight(name):
        slot, src, dst, axis = weights[name]
        pending[name] = [
            remote(
                half_of(src),
                half_of(dst(place[axis])),
                w_send.at[slot, step - 1],
                w_recv.at[slot, step - 1],
                dev(axis, step),
            )
            for step in (1, 3, 2)
        ]

    def forward_weight(name):
        slot, src, dst, axis = weights[name]
        passed = []
        for step, copy in zip((1, 3, 2), pending[name]):
            copy.wait_recv()
            block = half_of(dst((place[axis] - step + 4) % 4))
            passed.append(
                remote(
                    block,
                    block,
                    f_send.at[slot, step - 1],
                    f_recv.at[slot, step - 1],
                    sibling,
                )
            )
        pending[name] = passed

    def finish_weight(name):
        slot = weights[name][0]
        for copy in pending[name]:
            copy.wait_recv()
        local[slot].wait()

    local = []
    for slot, src, dst, axis in weights.values():
        copy = pltpu.make_async_copy(src, dst(place[axis]), local_sem.at[slot])
        copy.start()
        local.append(copy)

    resid = hidden[...].astype(F32)
    row = lax.broadcasted_iota(jnp.int32, (ROWS, 1), 0)
    is_text = me * ROWS + row < text_len[0]

    def modul(k):
        two = modulation[k]
        return jnp.where(is_text, two[0:1, :], two[1:2, :])

    normed = (layer_norm(resid, 1e-05) * (1.0 + modul(1)) + modul(0)).astype(BF)

    def gather_start(bufs, values, p, q):
        for buf, value, (one, two) in zip(bufs, values, ((p, q), (q, p))):
            for i, part in enumerate(value):
                lo = 0 if i == 0 else HALF
                buf[place[two], place[one], :, lo : lo + part.shape[1]] = part

    def gather_send(bufs, p, q, slot, phase):
        copies = []
        for h, (buf, (one, two)) in enumerate(zip(bufs, ((p, q), (q, p)))):
            for step in (1, 3, 2):
                ref = (
                    buf.at[place[two], place[one]] if phase == 0 else buf.at[place[two]]
                )
                copies.append(
                    remote(
                        ref,
                        ref,
                        c_send.at[slot, phase, h, step - 1],
                        c_recv.at[slot, phase, h, step - 1],
                        dev(one if phase == 0 else two, step),
                    )
                )
        return copies

    def gather_to_rows(bufs):
        for q_at in range(SIDE):
            for p_at in range(SIDE):
                at = (q_at * SIDE + p_at) * ROWS
                rows32[at : at + ROWS, 0:HALF] = bufs[0][q_at, p_at, :, 0:HALF].astype(F32)
                rows32[at : at + ROWS, HALF:D] = bufs[1][p_at, q_at, :, 0:HALF].astype(F32)

    gather_start(
        (ag1a, ag1b), ((normed[:, 0:HALF], pos[...]), (normed[:, HALF:D],)), "y", "z"
    )

    pl.semaphore_wait(barrier, len(everyone))

    first = gather_send((ag1a, ag1b), "y", "z", 0, 0)
    start_weight("qkv")
    for copy in first:
        copy.wait_recv()
    second = gather_send((ag1a, ag1b), "y", "z", 0, 1)

    lane_a = lax.broadcasted_iota(jnp.int32, (HC, HC), 0)
    lane_b = lax.broadcasted_iota(jnp.int32, (HC, HC), 1)
    average = jnp.where(lane_a // HD == lane_b // HD, 1.0 / HD, 0.0).astype(F32)
    turn = (
        jnp.where((lane_a == lane_b + 1) & (lane_b % 2 == 0), -1.0, 0.0)
        + jnp.where((lane_a + 1 == lane_b) & (lane_b % 2 == 1), 1.0, 0.0)
    ).astype(F32)
    key = lax.broadcasted_iota(jnp.int32, (64, 512), 1)
    owner = (key // 32) % 4 * 16 + (key // 8) % 4 * 4 + key // 128
    pick = jnp.where(lax.broadcasted_iota(jnp.int32, (64, 512), 0) == owner, 1.0, 0.0)
    count_of = exact_dot(
        jnp.broadcast_to(counts_row[...].astype(F32), (ROWS, 64)), pick.astype(F32)
    )
    key_row = lax.broadcasted_iota(jnp.int32, (ROWS, 512), 1) % ROWS
    live = jnp.where(key_row.astype(F32) < count_of, 1.0, 0.0)[0:1, :]
    dim = lax.broadcasted_iota(jnp.int32, (PAD, HC), 1) % HD
    which = jnp.where(dim < 16, 0, jnp.where(dim < 40, 1, 2))
    axis_of = jnp.where(
        lax.broadcasted_iota(jnp.int32, (PAD, HC), 0) == which, 1.0, 0.0
    ).astype(F32)

    for copy in second:
        copy.wait_recv()
    start_weight("out")
    start_weight("up")
    start_weight("down")
    gather_to_rows((ag1a, ag1b))
    for z_at in range(SIDE):
        for y_at in range(SIDE):
            at = (z_at * SIDE + y_at) * ROWS
            swap[at : at + ROWS, :] = ag1a[z_at, y_at, :, HALF : HALF + PAD].astype(F32)
    angles = exact_dot(swap[...], axis_of) * freq[...]
    cosine = jnp.cos(angles)
    sine = jnp.sin(angles)
    tokens = rows32[...].astype(BF)

    forward_weight("qkv")
    finish_weight("qkv")

    def heads(columns):
        values = columns.astype(BF).astype(F32)
        center = values - exact_dot(values, average)
        spread = exact_dot(center * center, average)
        unit = center * lax.rsqrt(spread + 1e-06)
        return unit * cosine + exact_dot(unit, turn) * sine

    def project(part):
        return dot_nt(tokens, wqkv[part].reshape(HC, D))

    keys = heads(project(1)).astype(BF)
    kv[x, :, 0:HC] = keys
    kv[x, :, HC : 2 * HC] = project(2).astype(BF)
    moved = [
        remote(
            kv.at[x],
            kv.at[x],
            c_send.at[4, 0, 0, step - 1],
            c_recv.at[4, 0, 0, step - 1],
            dev("x", step),
        )
        for step in (1, 3, 2)
    ]
    queries = (heads(project(0)) * HD ** (-0.5)).astype(BF)
    for copy in moved:
        copy.wait_recv()
    forward_weight("out")

    all_keys = kv[:, :, 0:HC].reshape(4 * 128, HC)
    all_values = kv[:, :, 128 : 2 * HC].reshape(4 * 128, 2 * HC - 128)
    lane_q = lax.broadcasted_iota(jnp.int32, (1, HC), 1) // HD
    lane_v = lax.broadcasted_iota(jnp.int32, (1, 256), 1) // HD - 1
    context = jnp.zeros((128, 256), F32)
    for head in range(HC // HD):
        chosen = jnp.where(lane_q == head, queries, jnp.zeros_like(queries))
        attend = jnp.exp(dot_nt(chosen, all_keys)) * live
        denom = jnp.sum(attend, axis=1, keepdims=True)
        numer = jnp.dot(attend.astype(BF), all_values, preferred_element_type=F32)
        context = jnp.where(lane_v == head, numer / denom, context)
    context = context[:, 64:256].astype(BF)
    finish_weight("out")

    def scatter_sum(send, recv, mid, last, produce, p, q, slot):
        order = ((q, p), (p, q))
        copies = [[], []]
        for h in range(2):
            part = produce(h)
            for q_at in range(SIDE):
                for p_at in range(SIDE):
                    at = (q_at * SIDE + p_at) * ROWS
                    i, j = (q_at, p_at) if h == 0 else (p_at, q_at)
                    send[h, i, j] = part[at : at + ROWS, :].astype(BF)
            for step in (1, 3, 2):
                one = order[h][0]
                copies[h].append(
                    remote(
                        send.at[h, (place[one] + step) % 4],
                        recv.at[h, step - 1],
                        c_send.at[slot, 0, h, step - 1],
                        c_recv.at[slot, 0, h, step - 1],
                        dev(one, step),
                    )
                )
        second = [[], []]
        for h in range(2):
            one, two = order[h]
            for copy in copies[h]:
                copy.wait_recv()
            for j in range(SIDE):
                total = send[h, place[one], j].astype(F32)
                for k in range(3):
                    total = total + recv[h, k, j].astype(F32)
                mid[h, j] = total.astype(BF)
            for step in (1, 3, 2):
                second[h].append(
                    remote(
                        mid.at[h, (place[two] + step) % 4],
                        last.at[h, step - 1],
                        c_send.at[slot, 1, h, step - 1],
                        c_recv.at[slot, 1, h, step - 1],
                        dev(two, step),
                    )
                )
        halves = []
        for h in range(2):
            one, two = order[h]
            for copy in second[h]:
                copy.wait_recv()
            total = mid[h, place[two]].astype(F32)
            for k in range(3):
                total = total + last[h, k].astype(F32)
            halves.append(total)
        return jnp.concatenate(halves, axis=1)

    out_weight = wout[...].reshape(HC, D)
    attended = scatter_sum(
        *rs1,
        lambda h: jnp.dot(
            context, out_weight[:, h * HALF : (h + 1) * HALF], preferred_element_type=F32
        ),
        "y",
        "z",
        1,
    )
    first_res = resid + modul(2) * attended
    normed_two = (layer_norm(first_res, 1e-05) * (1.0 + modul(4)) + modul(3)).astype(BF)
    gather_start(
        (ag2a, ag2b), ((normed_two[:, 0:HALF],), (normed_two[:, HALF:D],)), "x", "z"
    )
    for copy in gather_send((ag2a, ag2b), "x", "z", 2, 0):
        copy.wait_recv()
    second = gather_send((ag2a, ag2b), "x", "z", 2, 1)
    forward_weight("up")
    for copy in second:
        copy.wait_recv()
    gather_to_rows((ag2a, ag2b))
    tokens_two = rows32[...].astype(BF)
    finish_weight("up")
    inner = jax.nn.gelu(
        dot_nt(tokens_two, wup[...].reshape(SIDE * HID, D)), approximate=True
    ).astype(BF)
    forward_weight("down")
    finish_weight("down")
    down_weight = wdown[...].reshape(SIDE * HID, D)
    reduced = scatter_sum(
        *rs2,
        lambda h: jnp.dot(
            inner, down_weight[:, h * HALF : (h + 1) * HALF], preferred_element_type=F32
        ),
        "x",
        "z",
        3,
    )
    second_res = first_res + modul(5) * reduced
    final = (
        layer_norm(second_res, 1e-05) * (1.0 + out_mod[1:2, :]) + out_mod[0:1, :]
    ).astype(BF)
    prediction = dot_nt(final, w_proj[...])
    swap[0:ROWS, 0:64] = prediction
    other = remote(
        swap.at[0:ROWS], swap.at[ROWS : 2 * ROWS], c_send.at[4, 1, 0, 0], c_recv.at[4, 1, 0, 0], sibling
    )
    other.wait_recv()
    theirs = swap[ROWS : 2 * ROWS, 0:64]
    is_cond = cfg == 0
    pred_cond = jnp.where(is_cond, prediction, theirs)
    pred_uncond = jnp.where(is_cond, theirs, prediction)
    guided = pred_uncond + guidance[0] * (pred_cond - pred_uncond)
    guided = jnp.where(is_cond, guided[:, 0:32], guided[:, 32:64])
    updated = solver[0] * latent[...] + solver[1] * guided
    keep = (row < counts[me]) & jnp.logical_not(is_text)
    out[...] = jnp.where(keep, updated, latent[...])
    for copy in sends:
        copy.wait_send()


def shards(
    hidden,
    latent,
    positions,
    counts,
    text_len,
    modulation,
    w_qkv,
    w_out,
    w_up,
    w_down,
    out_mod,
    w_proj,
    guidance,
    solver,
):
    slots = lax.axis_index("seq") * ROWS + jnp.arange(ROWS)
    places = jnp.where((slots < text_len[0])[:, None], 0, positions).astype(BF)
    pos = jnp.pad(places, ((0, 0), (0, PAD - 3)))
    vmem = pl.BlockSpec(memory_space=pltpu.VMEM)
    smem = pl.BlockSpec(memory_space=pltpu.SMEM)
    whole = pl.BlockSpec(memory_space=pl.ANY)

    def sums():
        return (
            pltpu.VMEM((2, SIDE, SIDE, ROWS, HALF), BF),
            pltpu.VMEM((2, 3, SIDE, ROWS, HALF), BF),
            pltpu.VMEM((2, SIDE, ROWS, HALF), BF),
            pltpu.VMEM((2, 3, ROWS, HALF), BF),
        )

    return pl.pallas_call(
        kernel,
        out_shape=jax.ShapeDtypeStruct(latent.shape, F32),
        in_specs=[vmem, vmem, vmem, vmem, smem, smem, vmem, vmem]
        + [whole] * 4
        + [vmem, vmem, smem, smem],
        out_specs=vmem,
        scratch_shapes=[
            pltpu.VMEM((3, SIDE, 48, D), BF),
            pltpu.VMEM((SIDE, 48, D), BF),
            pltpu.VMEM((SIDE, HID, D), BF),
            pltpu.VMEM((SIDE, HID, D), BF),
            pltpu.VMEM((SIDE, SIDE, ROWS, HALF + PAD), BF),
            pltpu.VMEM((SIDE, SIDE, ROWS, HALF), BF),
            pltpu.VMEM((SIDE, SIDE, ROWS, HALF), BF),
            pltpu.VMEM((SIDE, SIDE, ROWS, HALF), BF),
            pltpu.VMEM((SIDE * SIDE * ROWS, D), F32),
            pltpu.VMEM((SIDE, SIDE * SIDE * ROWS, 2 * HC), BF),
            sums(),
            sums(),
            pltpu.VMEM((SIDE * SIDE * ROWS, PAD), F32),
            pltpu.SemaphoreType.DMA((4, 3)),
            pltpu.SemaphoreType.DMA((4, 3)),
            pltpu.SemaphoreType.DMA((4, 3)),
            pltpu.SemaphoreType.DMA((4, 3)),
            pltpu.SemaphoreType.DMA((4,)),
            pltpu.SemaphoreType.DMA((5, 2, 2, 3)),
            pltpu.SemaphoreType.DMA((5, 2, 2, 3)),
        ],
        compiler_params=pltpu.CompilerParams(
            collective_id=0, has_side_effects=True, vmem_limit_bytes=56 << 20
        ),
        name="step",
    )(
        hidden[0],
        latent,
        pos,
        counts[None, :],
        counts,
        text_len,
        modulation.transpose(1, 0, 2),
        jnp.asarray(frequencies()),
        w_qkv.transpose(1, 2, 0),
        w_out,
        w_up.T,
        w_down,
        out_mod,
        w_proj.T,
        guidance,
        solver,
    )


def solution(mesh):
    in_specs = (
        P("cfg", "seq", None),
        P("seq", "cfg"),
        P("seq", None),
        P(),
        P(),
        P(),
        P(None, None, "seq"),
        P("seq", None),
        P(None, "seq"),
        P("seq", None),
        P(),
        P(),
        P(),
        P(),
    )
    return jax.shard_map(
        shards, mesh=mesh, in_specs=in_specs, out_specs=P("seq", "cfg"), check_vma=False
    )
```

```python
import functools

import jax
import jax.numpy as jnp
import numpy as np
from jax import lax
from jax.experimental import pallas as pl
from jax.experimental.pallas import tpu as pltpu
from jax.sharding import PartitionSpec as P

D = 3072
HD = 64
SIDE = 4
ROWS = 8
HALF = D // 2
HC = 192
HID = 192
PAD = 128
BF = jnp.bfloat16
F32 = jnp.float32
NT = (((1,), (1,)), ((), ()))


def layer_norm(values, epsilon):
    center = values - jnp.mean(values, axis=-1, keepdims=True)
    spread = jnp.mean(center * center, axis=-1, keepdims=True)
    return center * lax.rsqrt(spread + epsilon)


def dot_nt(a, b):
    return lax.dot_general(a, b, NT, preferred_element_type=F32)


def exact_dot(a, b):
    return lax.dot_general(
        a,
        b,
        (((1,), (0,)), ((), ())),
        preferred_element_type=F32,
        precision=lax.Precision.HIGHEST,
    )


def frequencies():
    frame = 10000.0 ** (-2.0 * np.arange(8) / 16)
    side = 10000.0 ** (-2.0 * np.arange(12) / 24)
    pairs = np.concatenate([frame, side, side])
    return np.tile(np.repeat(pairs, 2), 3)[None, :].astype(np.float32)


def kernel(
    latent,
    counts_row,
    freq,
    positions,
    counts,
    text_len,
    guidance,
    solver,
    hidden_far,
    modulation_far,
    out_mod_far,
    w_proj_far,
    w_qkv,
    w_out,
    w_up,
    w_down,
    out,
    hidden,
    modulation,
    out_mod,
    w_proj,
    wqkv,
    wout,
    wup,
    wdown,
    ag1a,
    ag1b,
    ag2a,
    ag2b,
    rows32,
    kv,
    rs1,
    rs2,
    swap,
    w_send,
    w_recv,
    near_sem,
    local_sem,
    c_send,
    c_recv,
):
    cfg = lax.axis_index("cfg")
    me = lax.axis_index("seq")
    z, y, x = me // 16, (me // 4) % 4, me % 4

    def dev(axis, step):
        zz = (z + step) % 4 if axis == "z" else z
        yy = (y + step) % 4 if axis == "y" else y
        xx = (x + step) % 4 if axis == "x" else x
        return (cfg, zz * 16 + yy * 4 + xx)

    place = {"x": x, "y": y, "z": z}
    sibling = (1 - cfg, me)
    sends = []

    def remote(src, dst, send, recv, device):
        copy = pltpu.make_async_remote_copy(
            src_ref=src,
            dst_ref=dst,
            send_sem=send,
            recv_sem=recv,
            device_id=device,
            device_id_type=pl.DeviceIdType.MESH,
        )
        copy.start()
        sends.append(copy)
        return copy

    barrier = pltpu.get_barrier_semaphore()
    everyone = [dev(axis, step) for axis in "xyz" for step in (1, 2, 3)] + [sibling]
    for device in everyone:
        pl.semaphore_signal(
            barrier, inc=1, device_id=device, device_id_type=pl.DeviceIdType.MESH
        )

    near = []
    for i, (far, ref) in enumerate(
        (
            (hidden_far, hidden),
            (modulation_far, modulation),
            (out_mod_far, out_mod),
            (w_proj_far, w_proj),
        )
    ):
        copy = pltpu.make_async_copy(far, ref, near_sem.at[i])
        copy.start()
        near.append(copy)

    weights = {
        "k": (0, w_qkv.at[1], lambda i: wqkv.at[1, i], "x"),
        "v": (1, w_qkv.at[2], lambda i: wqkv.at[2, i], "x"),
        "q": (2, w_qkv.at[0], lambda i: wqkv.at[0, i], "x"),
        "out": (3, w_out, lambda i: wout.at[i], "x"),
        "up": (4, w_up, lambda i: wup.at[i], "y"),
        "down": (5, w_down, lambda i: wdown.at[i], "y"),
    }
    start = pl.multiple_of(cfg * HALF, HALF)
    half = pl.ds(start, HALF)
    quarters = (
        pl.ds(start, HALF // 2),
        pl.ds(pl.multiple_of(start + HALF // 2, HALF // 2), HALF // 2),
    )
    turns = (1, 3)
    moving = {}
    local = []

    def send_weight(name):
        slot, src, dst, axis = weights[name]
        moving[name, 0] = [
            remote(
                src.at[:, half],
                dst(place[axis]).at[:, half],
                w_send.at[slot, 0, i],
                w_recv.at[slot, 0, i],
                dev(axis, turn),
            )
            for i, turn in enumerate(turns)
        ]

    def pass_weight(name):
        slot, src, dst, axis = weights[name]
        moving[name, 1], moving[name, 2] = [], []
        for i, turn in enumerate(turns):
            moving[name, 0][i].wait_recv()
            block = dst((place[axis] - turn + 4) % 4)
            moving[name, 1].append(
                remote(
                    block.at[:, quarters[i]],
                    block.at[:, quarters[i]],
                    w_send.at[slot, 1, i],
                    w_recv.at[slot, 1, i],
                    dev(axis, turn),
                )
            )
            moving[name, 2].append(
                remote(
                    block.at[:, half],
                    block.at[:, half],
                    w_send.at[slot, 2, i],
                    w_recv.at[slot, 2, i],
                    sibling,
                )
            )

    def end_weight(name):
        slot, src, dst, axis = weights[name]
        for copy in moving[name, 1]:
            copy.wait_recv()
        block = dst((place[axis] + 2) % 4)
        moving[name, 2].append(
            remote(
                block.at[:, half],
                block.at[:, half],
                w_send.at[slot, 3, 0],
                w_recv.at[slot, 3, 0],
                sibling,
            )
        )

    def have_weight(name):
        for copy in moving[name, 2]:
            copy.wait_recv()
        local[weights[name][0]].wait()

    near[0].wait()
    near[1].wait()
    resid = hidden[...].astype(F32)
    row = lax.broadcasted_iota(jnp.int32, (ROWS, 1), 0)
    is_text = me * ROWS + row < text_len[0]

    def modul(k):
        two = modulation[k]
        return jnp.where(is_text, two[0:1, :], two[1:2, :])

    normed = (layer_norm(resid, 1e-05) * (1.0 + modul(1)) + modul(0)).astype(BF)

    def gather_start(bufs, values, p, q):
        for buf, value, (one, two) in zip(bufs, values, ((p, q), (q, p))):
            for i, part in enumerate(value):
                lo = 0 if i == 0 else HALF
                buf[place[two], place[one], :, lo : lo + part.shape[1]] = part

    def gather_send(bufs, p, q, slot, phase):
        copies = []
        for h, (buf, (one, two)) in enumerate(zip(bufs, ((p, q), (q, p)))):
            for step in (1, 3, 2):
                ref = (
                    buf.at[place[two], place[one]] if phase == 0 else buf.at[place[two]]
                )
                copies.append(
                    remote(
                        ref,
                        ref,
                        c_send.at[slot, phase, h, step - 1],
                        c_recv.at[slot, phase, h, step - 1],
                        dev(one if phase == 0 else two, step),
                    )
                )
        return copies

    def gather_to_rows(bufs):
        for q_at in range(SIDE):
            for p_at in range(SIDE):
                at = (q_at * SIDE + p_at) * ROWS
                rows32[at : at + ROWS, 0:HALF] = bufs[0][q_at, p_at, :, 0:HALF].astype(F32)
                rows32[at : at + ROWS, HALF:D] = bufs[1][p_at, q_at, :, 0:HALF].astype(F32)

    lane = lax.broadcasted_iota(jnp.int32, (ROWS, PAD), 1)
    line = lax.broadcasted_iota(jnp.int32, (ROWS, PAD), 0)
    pos = jnp.zeros((ROWS, PAD), F32)
    for k in range(3):
        for r in range(ROWS):
            at = positions[k, r].astype(F32)
            pos = jnp.where((lane == k) & (line == r), at, pos)
    pos = jnp.where(is_text, 0.0, pos).astype(BF)
    gather_start(
        (ag1a, ag1b), ((normed[:, 0:HALF], pos), (normed[:, HALF:D],)), "y", "z"
    )

    pl.semaphore_wait(barrier, len(everyone))

    first = gather_send((ag1a, ag1b), "y", "z", 0, 0)
    for name in ("k", "v", "q", "out"):
        send_weight(name)
    for slot, src, dst, axis in weights.values():
        copy = pltpu.make_async_copy(src, dst(place[axis]), local_sem.at[slot])
        copy.start()
        local.append(copy)
    for copy in first:
        copy.wait_recv()
    second = gather_send((ag1a, ag1b), "y", "z", 0, 1)
    send_weight("up")
    send_weight("down")

    lane_a = lax.broadcasted_iota(jnp.int32, (HC, HC), 0)
    lane_b = lax.broadcasted_iota(jnp.int32, (HC, HC), 1)
    average = jnp.where(lane_a // HD == lane_b // HD, 1.0 / HD, 0.0).astype(F32)
    turn = (
        jnp.where((lane_a == lane_b + 1) & (lane_b % 2 == 0), -1.0, 0.0)
        + jnp.where((lane_a + 1 == lane_b) & (lane_b % 2 == 1), 1.0, 0.0)
    ).astype(F32)
    key = lax.broadcasted_iota(jnp.int32, (64, 512), 1)
    owner = (key // 32) % 4 * 16 + (key // 8) % 4 * 4 + key // 128
    pick = jnp.where(lax.broadcasted_iota(jnp.int32, (64, 512), 0) == owner, 1.0, 0.0)
    count_of = exact_dot(
        jnp.broadcast_to(counts_row[...].astype(F32), (ROWS, 64)), pick.astype(F32)
    )
    key_row = lax.broadcasted_iota(jnp.int32, (ROWS, 512), 1) % ROWS
    live = jnp.where(key_row.astype(F32) < count_of, 1.0, 0.0)[0:1, :]
    dim = lax.broadcasted_iota(jnp.int32, (PAD, HC), 1) % HD
    which = jnp.where(dim < 16, 0, jnp.where(dim < 40, 1, 2))
    axis_of = jnp.where(
        lax.broadcasted_iota(jnp.int32, (PAD, HC), 0) == which, 1.0, 0.0
    ).astype(F32)

    for name in ("k", "v", "q"):
        pass_weight(name)
    for copy in second:
        copy.wait_recv()
    gather_to_rows((ag1a, ag1b))
    for z_at in range(SIDE):
        for y_at in range(SIDE):
            at = (z_at * SIDE + y_at) * ROWS
            swap[at : at + ROWS, :] = ag1a[z_at, y_at, :, HALF : HALF + PAD].astype(F32)
    angles = exact_dot(swap[...], axis_of) * freq[...]
    cosine = jnp.cos(angles)
    sine = jnp.sin(angles)
    tokens = rows32[...].astype(BF)

    pass_weight("out")
    for name in ("k", "v", "q"):
        end_weight(name)

    def heads(columns):
        values = columns.astype(BF).astype(F32)
        center = values - exact_dot(values, average)
        spread = exact_dot(center * center, average)
        unit = center * lax.rsqrt(spread + 1e-06)
        return unit * cosine + exact_dot(unit, turn) * sine

    def project(part):
        return dot_nt(tokens, wqkv[part].reshape(HC, D))

    have_weight("k")
    keys = heads(project(1)).astype(BF)
    have_weight("v")
    kv[x, :, 0:HC] = keys
    kv[x, :, HC : 2 * HC] = project(2).astype(BF)
    moved = [
        remote(
            kv.at[x],
            kv.at[x],
            c_send.at[4, 0, 0, step - 1],
            c_recv.at[4, 0, 0, step - 1],
            dev("x", step),
        )
        for step in (1, 3, 2)
    ]
    have_weight("q")
    queries = (heads(project(0)) * HD ** (-0.5)).astype(BF)
    for copy in moved:
        copy.wait_recv()
    end_weight("out")

    all_keys = kv[:, :, 0:HC].reshape(4 * 128, HC)
    all_values = kv[:, :, 128 : 2 * HC].reshape(4 * 128, 2 * HC - 128)
    lane_q = lax.broadcasted_iota(jnp.int32, (1, HC), 1) // HD
    lane_v = lax.broadcasted_iota(jnp.int32, (1, 256), 1) // HD - 1
    context = jnp.zeros((128, 256), F32)
    for head in range(HC // HD):
        chosen = jnp.where(lane_q == head, queries, jnp.zeros_like(queries))
        attend = jnp.exp(dot_nt(chosen, all_keys)) * live
        denom = jnp.sum(attend, axis=1, keepdims=True)
        numer = jnp.dot(attend.astype(BF), all_values, preferred_element_type=F32)
        context = jnp.where(lane_v == head, numer / denom, context)
    context = context[:, 64:256].astype(BF)
    have_weight("out")

    def scatter_sum(send, recv, mid, last, produce, p, q, slot, meanwhile):
        order = ((q, p), (p, q))
        copies = [[], []]
        for h in range(2):
            part = produce(h)
            for q_at in range(SIDE):
                for p_at in range(SIDE):
                    at = (q_at * SIDE + p_at) * ROWS
                    i, j = (q_at, p_at) if h == 0 else (p_at, q_at)
                    send[h, i, j] = part[at : at + ROWS, :].astype(BF)
            for step in (1, 3, 2):
                one = order[h][0]
                copies[h].append(
                    remote(
                        send.at[h, (place[one] + step) % 4],
                        recv.at[h, step - 1],
                        c_send.at[slot, 0, h, step - 1],
                        c_recv.at[slot, 0, h, step - 1],
                        dev(one, step),
                    )
                )
        meanwhile()
        second = [[], []]
        for h in range(2):
            one, two = order[h]
            for copy in copies[h]:
                copy.wait_recv()
            for j in range(SIDE):
                total = send[h, place[one], j].astype(F32)
                for k in range(3):
                    total = total + recv[h, k, j].astype(F32)
                mid[h, j] = total.astype(BF)
            for step in (1, 3, 2):
                second[h].append(
                    remote(
                        mid.at[h, (place[two] + step) % 4],
                        last.at[h, step - 1],
                        c_send.at[slot, 1, h, step - 1],
                        c_recv.at[slot, 1, h, step - 1],
                        dev(two, step),
                    )
                )
        halves = []
        for h in range(2):
            one, two = order[h]
            for copy in second[h]:
                copy.wait_recv()
            total = mid[h, place[two]].astype(F32)
            for k in range(3):
                total = total + last[h, k].astype(F32)
            halves.append(total)
        return jnp.concatenate(halves, axis=1)

    out_weight = wout[...].reshape(HC, D)
    attended = scatter_sum(
        *rs1,
        lambda h: jnp.dot(
            context, out_weight[:, h * HALF : (h + 1) * HALF], preferred_element_type=F32
        ),
        "y",
        "z",
        1,
        lambda: pass_weight("up"),
    )
    first_res = resid + modul(2) * attended
    normed_two = (layer_norm(first_res, 1e-05) * (1.0 + modul(4)) + modul(3)).astype(BF)
    gather_start(
        (ag2a, ag2b), ((normed_two[:, 0:HALF],), (normed_two[:, HALF:D],)), "x", "z"
    )
    for copy in gather_send((ag2a, ag2b), "x", "z", 2, 0):
        copy.wait_recv()
    second = gather_send((ag2a, ag2b), "x", "z", 2, 1)
    pass_weight("down")
    end_weight("up")
    for copy in second:
        copy.wait_recv()
    gather_to_rows((ag2a, ag2b))
    tokens_two = rows32[...].astype(BF)
    end_weight("down")
    have_weight("up")
    inner = jax.nn.gelu(
        dot_nt(tokens_two, wup[...].reshape(SIDE * HID, D)), approximate=True
    ).astype(BF)
    have_weight("down")
    down_weight = wdown[...].reshape(SIDE * HID, D)
    reduced = scatter_sum(
        *rs2,
        lambda h: jnp.dot(
            inner, down_weight[:, h * HALF : (h + 1) * HALF], preferred_element_type=F32
        ),
        "x",
        "z",
        3,
        lambda: None,
    )
    near[2].wait()
    near[3].wait()
    second_res = first_res + modul(5) * reduced
    final = (
        layer_norm(second_res, 1e-05) * (1.0 + out_mod[1:2, :]) + out_mod[0:1, :]
    ).astype(BF)
    prediction = dot_nt(final, w_proj[...])
    swap[0:ROWS, 0:64] = prediction
    other = remote(
        swap.at[0:ROWS], swap.at[ROWS : 2 * ROWS], c_send.at[4, 1, 0, 0], c_recv.at[4, 1, 0, 0], sibling
    )
    other.wait_recv()
    theirs = swap[ROWS : 2 * ROWS, 0:64]
    is_cond = cfg == 0
    pred_cond = jnp.where(is_cond, prediction, theirs)
    pred_uncond = jnp.where(is_cond, theirs, prediction)
    guided = pred_uncond + guidance[0] * (pred_cond - pred_uncond)
    guided = jnp.where(is_cond, guided[:, 0:32], guided[:, 32:64])
    updated = solver[0] * latent[...] + solver[1] * guided
    keep = (row < counts[me]) & jnp.logical_not(is_text)
    out[...] = jnp.where(keep, updated, latent[...])
    for copy in sends:
        copy.wait_send()


def shards(
    hidden,
    latent,
    positions,
    counts,
    text_len,
    modulation,
    w_qkv,
    w_out,
    w_up,
    w_down,
    out_mod,
    w_proj,
    guidance,
    solver,
):
    vmem = pl.BlockSpec(memory_space=pltpu.VMEM)
    smem = pl.BlockSpec(memory_space=pltpu.SMEM)
    whole = pl.BlockSpec(memory_space=pl.ANY)

    def sums():
        return (
            pltpu.VMEM((2, SIDE, SIDE, ROWS, HALF), BF),
            pltpu.VMEM((2, 3, SIDE, ROWS, HALF), BF),
            pltpu.VMEM((2, SIDE, ROWS, HALF), BF),
            pltpu.VMEM((2, 3, ROWS, HALF), BF),
        )

    return pl.pallas_call(
        kernel,
        out_shape=jax.ShapeDtypeStruct(latent.shape, F32),
        in_specs=[vmem] * 3 + [smem] * 5 + [whole] * 8,
        out_specs=vmem,
        scratch_shapes=[
            pltpu.VMEM((ROWS, D), BF),
            pltpu.VMEM((6, 2, D), F32),
            pltpu.VMEM((2, D), F32),
            pltpu.VMEM((64, D), BF),
            pltpu.VMEM((3, SIDE, 48, D), BF),
            pltpu.VMEM((SIDE, 48, D), BF),
            pltpu.VMEM((SIDE, HID, D), BF),
            pltpu.VMEM((SIDE, HID, D), BF),
            pltpu.VMEM((SIDE, SIDE, ROWS, HALF + PAD), BF),
            pltpu.VMEM((SIDE, SIDE, ROWS, HALF), BF),
            pltpu.VMEM((SIDE, SIDE, ROWS, HALF), BF),
            pltpu.VMEM((SIDE, SIDE, ROWS, HALF), BF),
            pltpu.VMEM((SIDE * SIDE * ROWS, D), F32),
            pltpu.VMEM((SIDE, SIDE * SIDE * ROWS, 2 * HC), BF),
            sums(),
            sums(),
            pltpu.VMEM((SIDE * SIDE * ROWS, PAD), F32),
            pltpu.SemaphoreType.DMA((6, 4, 2)),
            pltpu.SemaphoreType.DMA((6, 4, 2)),
            pltpu.SemaphoreType.DMA((4,)),
            pltpu.SemaphoreType.DMA((6,)),
            pltpu.SemaphoreType.DMA((5, 2, 2, 3)),
            pltpu.SemaphoreType.DMA((5, 2, 2, 3)),
        ],
        compiler_params=pltpu.CompilerParams(
            collective_id=0, has_side_effects=True, vmem_limit_bytes=56 << 20
        ),
        name="step",
    )(
        latent,
        counts[None, :],
        jnp.asarray(frequencies()),
        positions.T,
        counts,
        text_len,
        guidance,
        solver,
        hidden[0],
        modulation.transpose(1, 0, 2),
        out_mod,
        w_proj.T,
        w_qkv.transpose(1, 2, 0),
        w_out,
        w_up.T,
        w_down,
    )


def solution(mesh):
    in_specs = (
        P("cfg", "seq", None),
        P("seq", "cfg"),
        P("seq", None),
        P(),
        P(),
        P(),
        P(None, None, "seq"),
        P("seq", None),
        P(None, "seq"),
        P("seq", None),
        P(),
        P(),
        P(),
        P(),
    )
    return jax.shard_map(
        shards, mesh=mesh, in_specs=in_specs, out_specs=P("seq", "cfg"), check_vma=False
    )
```

```python
import functools

import jax
import jax.numpy as jnp
import numpy as np
from jax import lax
from jax.experimental import pallas as pl
from jax.experimental.pallas import tpu as pltpu
from jax.sharding import PartitionSpec as P

D = 3072
HD = 64
SIDE = 4
ROWS = 8
HALF = D // 2
HC = 192
HID = 192
PAD = 128
BF = jnp.bfloat16
F32 = jnp.float32
NT = (((1,), (1,)), ((), ()))


def layer_norm(values, epsilon):
    center = values - jnp.mean(values, axis=-1, keepdims=True)
    spread = jnp.mean(center * center, axis=-1, keepdims=True)
    return center * lax.rsqrt(spread + epsilon)


def dot_nt(a, b):
    return lax.dot_general(a, b, NT, preferred_element_type=F32)


def exact_dot(a, b):
    return lax.dot_general(
        a,
        b,
        (((1,), (0,)), ((), ())),
        preferred_element_type=F32,
        precision=lax.Precision.HIGHEST,
    )


def frequencies():
    frame = 10000.0 ** (-2.0 * np.arange(8) / 16)
    side = 10000.0 ** (-2.0 * np.arange(12) / 24)
    pairs = np.concatenate([frame, side, side])
    return np.tile(np.repeat(pairs, 2), 3)[None, :].astype(np.float32)


def kernel(
    latent,
    counts_row,
    freq,
    positions,
    counts,
    text_len,
    guidance,
    solver,
    hidden_far,
    modulation_far,
    out_mod_far,
    w_proj_far,
    w_qkv,
    w_out,
    w_up,
    w_down,
    out,
    hidden,
    modulation,
    out_mod,
    w_proj,
    wqkv,
    wout,
    wup,
    wdown,
    ag1a,
    ag1b,
    ag2a,
    ag2b,
    rows32,
    kv,
    rs1,
    rs2,
    swap,
    w_send,
    w_recv,
    near_sem,
    local_sem,
    c_send,
    c_recv,
    g_send,
    g_recv,
):
    cfg = lax.axis_index("cfg")
    me = lax.axis_index("seq")
    z, y, x = me // 16, (me // 4) % 4, me % 4

    def dev(axis, step):
        zz = (z + step) % 4 if axis == "z" else z
        yy = (y + step) % 4 if axis == "y" else y
        xx = (x + step) % 4 if axis == "x" else x
        return (cfg, zz * 16 + yy * 4 + xx)

    place = {"x": x, "y": y, "z": z}
    sibling = (1 - cfg, me)
    sends = []

    def remote(src, dst, send, recv, device):
        copy = pltpu.make_async_remote_copy(
            src_ref=src,
            dst_ref=dst,
            send_sem=send,
            recv_sem=recv,
            device_id=device,
            device_id_type=pl.DeviceIdType.MESH,
        )
        copy.start()
        sends.append(copy)
        return copy

    barrier = pltpu.get_barrier_semaphore()
    everyone = [dev(axis, step) for axis in "xyz" for step in (1, 2, 3)] + [sibling]
    for device in everyone:
        pl.semaphore_signal(
            barrier, inc=1, device_id=device, device_id_type=pl.DeviceIdType.MESH
        )

    near = []
    for i, (far, ref) in enumerate(
        (
            (hidden_far, hidden),
            (modulation_far, modulation),
            (out_mod_far, out_mod),
            (w_proj_far, w_proj),
        )
    ):
        copy = pltpu.make_async_copy(far, ref, near_sem.at[i])
        copy.start()
        near.append(copy)

    top, bottom = pl.ds(0, HID // 2), pl.ds(HID // 2, HID // 2)
    weights = {
        "k": (0, w_qkv.at[1], lambda i: wqkv.at[1, i], "x"),
        "v": (1, w_qkv.at[2], lambda i: wqkv.at[2, i], "x"),
        "q": (2, w_qkv.at[0], lambda i: wqkv.at[0, i], "x"),
        "out": (3, w_out, lambda i: wout.at[i], "x"),
        "up0": (4, w_up.at[top], lambda i: wup.at[i, top], "y"),
        "up1": (5, w_up.at[bottom], lambda i: wup.at[i, bottom], "y"),
        "down0": (6, w_down.at[top], lambda i: wdown.at[i, top], "y"),
        "down1": (7, w_down.at[bottom], lambda i: wdown.at[i, bottom], "y"),
    }
    start = pl.multiple_of(cfg * HALF, HALF)
    half = pl.ds(start, HALF)
    quarters = (
        pl.ds(start, HALF // 2),
        pl.ds(pl.multiple_of(start + HALF // 2, HALF // 2), HALF // 2),
    )
    turns = (1, 3)
    moving = {}
    local = []

    def send_weight(name):
        slot, src, dst, axis = weights[name]
        moving[name, 0] = [
            remote(
                src.at[:, half],
                dst(place[axis]).at[:, half],
                w_send.at[slot, 0, i],
                w_recv.at[slot, 0, i],
                dev(axis, turn),
            )
            for i, turn in enumerate(turns)
        ]

    def pass_weight(name):
        slot, src, dst, axis = weights[name]
        moving[name, 1], moving[name, 2] = [], []
        for i, turn in enumerate(turns):
            moving[name, 0][i].wait_recv()
            block = dst((place[axis] - turn + 4) % 4)
            moving[name, 1].append(
                remote(
                    block.at[:, quarters[i]],
                    block.at[:, quarters[i]],
                    w_send.at[slot, 1, i],
                    w_recv.at[slot, 1, i],
                    dev(axis, turn),
                )
            )
            moving[name, 2].append(
                remote(
                    block.at[:, half],
                    block.at[:, half],
                    w_send.at[slot, 2, i],
                    w_recv.at[slot, 2, i],
                    sibling,
                )
            )

    def end_weight(name):
        slot, src, dst, axis = weights[name]
        for copy in moving[name, 1]:
            copy.wait_recv()
        block = dst((place[axis] + 2) % 4)
        moving[name, 2].append(
            remote(
                block.at[:, half],
                block.at[:, half],
                w_send.at[slot, 3, 0],
                w_recv.at[slot, 3, 0],
                sibling,
            )
        )

    def have_weight(name):
        for copy in moving[name, 2]:
            copy.wait_recv()
        local[weights[name][0]].wait()

    near[0].wait()
    near[1].wait()
    resid = hidden[...].astype(F32)
    row = lax.broadcasted_iota(jnp.int32, (ROWS, 1), 0)
    is_text = me * ROWS + row < text_len[0]

    def modul(k):
        two = modulation[k]
        return jnp.where(is_text, two[0:1, :], two[1:2, :])

    normed = (layer_norm(resid, 1e-05) * (1.0 + modul(1)) + modul(0)).astype(BF)

    def gather_own(bufs, values, orders):
        for buf, value, (p, q) in zip(bufs, values, orders):
            for i, part in enumerate(value):
                lo = 0 if i == 0 else HALF
                buf[place[q], place[p], :, lo : lo + part.shape[1]] = part

    def gather_first(bufs, orders, slot):
        first = []
        for h, (buf, (p, q)) in enumerate(zip(bufs, orders)):
            ref = buf.at[place[q], place[p]]
            first.append(
                [
                    remote(
                        ref,
                        ref,
                        g_send.at[slot, h, 0, step - 1],
                        g_recv.at[slot, h, 0, step - 1],
                        dev(p, step),
                    )
                    for step in (1, 3, 2)
                ]
            )
        return first, [gather_pass(bufs[h], orders[h], slot, h, 0) for h in range(2)]

    def gather_pass(buf, order, slot, h, behind):
        p, q = order
        ref = buf.at[place[q], (place[p] - behind + 4) % 4]
        return [
            remote(
                ref,
                ref,
                g_send.at[slot, h, behind + 1, step - 1],
                g_recv.at[slot, h, behind + 1, step - 1],
                dev(q, step),
            )
            for step in (1, 3, 2)
        ]

    def gather_second(bufs, orders, slot, state):
        first, second = state
        for i, behind in enumerate((1, 3, 2)):
            for h in range(2):
                first[h][i].wait_recv()
                second[h] += gather_pass(bufs[h], orders[h], slot, h, behind)

    def gather_end(bufs, orders, outer, state):
        for copy in state[1][0] + state[1][1]:
            copy.wait_recv()
        for h, (buf, (p, q)) in enumerate(zip(bufs, orders)):
            for i in range(SIDE):
                for j in range(SIDE):
                    at = (i * SIDE + j if q == outer else j * SIDE + i) * ROWS
                    rows32[at : at + ROWS, h * HALF : (h + 1) * HALF] = buf[
                        i, j, :, 0:HALF
                    ].astype(F32)

    lane = lax.broadcasted_iota(jnp.int32, (ROWS, PAD), 1)
    line = lax.broadcasted_iota(jnp.int32, (ROWS, PAD), 0)
    pos = jnp.zeros((ROWS, PAD), F32)
    for k in range(3):
        for r in range(ROWS):
            at = positions[k, r].astype(F32)
            pos = jnp.where((lane == k) & (line == r), at, pos)
    pos = jnp.where(is_text, 0.0, pos).astype(BF)
    order_one = (("y", "z"), ("y", "z"))
    bufs_one = (ag1a, ag1b)
    gather_own(
        bufs_one, ((normed[:, 0:HALF], pos), (normed[:, HALF:D],)), order_one
    )

    pl.semaphore_wait(barrier, len(everyone))

    state = gather_first(bufs_one, order_one, 0)
    for name in ("k", "v", "up0", "up1"):
        send_weight(name)
    for slot, src, dst, axis in weights.values():
        copy = pltpu.make_async_copy(src, dst(place[axis]), local_sem.at[slot])
        copy.start()
        local.append(copy)
    gather_second(bufs_one, order_one, 0, state)
    pass_weight("k")
    pass_weight("v")
    send_weight("q")
    send_weight("out")

    lane_a = lax.broadcasted_iota(jnp.int32, (HC, HC), 0)
    lane_b = lax.broadcasted_iota(jnp.int32, (HC, HC), 1)
    average = jnp.where(lane_a // HD == lane_b // HD, 1.0 / HD, 0.0).astype(F32)
    turn = (
        jnp.where((lane_a == lane_b + 1) & (lane_b % 2 == 0), -1.0, 0.0)
        + jnp.where((lane_a + 1 == lane_b) & (lane_b % 2 == 1), 1.0, 0.0)
    ).astype(F32)
    key = lax.broadcasted_iota(jnp.int32, (64, 512), 1)
    owner = (key // 32) % 4 * 16 + (key // 8) % 4 * 4 + key // 128
    pick = jnp.where(lax.broadcasted_iota(jnp.int32, (64, 512), 0) == owner, 1.0, 0.0)
    count_of = exact_dot(
        jnp.broadcast_to(counts_row[...].astype(F32), (ROWS, 64)), pick.astype(F32)
    )
    key_row = lax.broadcasted_iota(jnp.int32, (ROWS, 512), 1) % ROWS
    live = jnp.where(key_row.astype(F32) < count_of, 1.0, 0.0)[0:1, :]
    dim = lax.broadcasted_iota(jnp.int32, (PAD, HC), 1) % HD
    which = jnp.where(dim < 16, 0, jnp.where(dim < 40, 1, 2))
    axis_of = jnp.where(
        lax.broadcasted_iota(jnp.int32, (PAD, HC), 0) == which, 1.0, 0.0
    ).astype(F32)

    end_weight("k")
    end_weight("v")
    pass_weight("up0")
    send_weight("down0")
    pass_weight("q")
    gather_end(bufs_one, order_one, "z", state)
    for z_at in range(SIDE):
        for y_at in range(SIDE):
            at = (z_at * SIDE + y_at) * ROWS
            swap[at : at + ROWS, :] = ag1a[z_at, y_at, :, HALF : HALF + PAD].astype(F32)
    angles = exact_dot(swap[...], axis_of) * freq[...]
    cosine = jnp.cos(angles)
    sine = jnp.sin(angles)
    tokens = rows32[...].astype(BF)

    pass_weight("up1")

    def heads(columns):
        values = columns.astype(BF).astype(F32)
        center = values - exact_dot(values, average)
        spread = exact_dot(center * center, average)
        unit = center * lax.rsqrt(spread + 1e-06)
        return unit * cosine + exact_dot(unit, turn) * sine

    def project(part):
        return dot_nt(tokens, wqkv[part].reshape(HC, D))

    have_weight("k")
    keys = heads(project(1)).astype(BF)
    have_weight("v")
    kv[x, :, 0:HC] = keys
    kv[x, :, HC : 2 * HC] = project(2).astype(BF)
    moved = [
        remote(
            kv.at[x],
            kv.at[x],
            c_send.at[4, 0, 0, step - 1],
            c_recv.at[4, 0, 0, step - 1],
            dev("x", step),
        )
        for step in (1, 3, 2)
    ]
    end_weight("q")
    pass_weight("out")
    have_weight("q")
    queries = (heads(project(0)) * HD ** (-0.5)).astype(BF)
    for copy in moved:
        copy.wait_recv()
    end_weight("out")

    all_keys = kv[:, :, 0:HC].reshape(4 * 128, HC)
    all_values = kv[:, :, 128 : 2 * HC].reshape(4 * 128, 2 * HC - 128)
    lane_q = lax.broadcasted_iota(jnp.int32, (1, HC), 1) // HD
    lane_v = lax.broadcasted_iota(jnp.int32, (1, 256), 1) // HD - 1
    context = jnp.zeros((128, 256), F32)
    for head in range(HC // HD):
        chosen = jnp.where(lane_q == head, queries, jnp.zeros_like(queries))
        attend = jnp.exp(dot_nt(chosen, all_keys)) * live
        denom = jnp.sum(attend, axis=1, keepdims=True)
        numer = jnp.dot(attend.astype(BF), all_values, preferred_element_type=F32)
        context = jnp.where(lane_v == head, numer / denom, context)
    context = context[:, 64:256].astype(BF)
    have_weight("out")

    def scatter_sum(send, recv, mid, last, produce, p, q, slot, hooks):
        order = ((q, p), (p, q))
        copies = [[], []]
        for h in range(2):
            part = produce(h)
            for q_at in range(SIDE):
                for p_at in range(SIDE):
                    at = (q_at * SIDE + p_at) * ROWS
                    i, j = (q_at, p_at) if h == 0 else (p_at, q_at)
                    send[h, i, j] = part[at : at + ROWS, :].astype(BF)
            for step in (1, 3, 2):
                one = order[h][0]
                copies[h].append(
                    remote(
                        send.at[h, (place[one] + step) % 4],
                        recv.at[h, step - 1],
                        c_send.at[slot, 0, h, step - 1],
                        c_recv.at[slot, 0, h, step - 1],
                        dev(one, step),
                    )
                )
        hooks[0]()
        second = [[], []]
        for h in range(2):
            one, two = order[h]
            for copy in copies[h]:
                copy.wait_recv()
            for j in range(SIDE):
                total = send[h, place[one], j].astype(F32)
                for k in range(3):
                    total = total + recv[h, k, j].astype(F32)
                mid[h, j] = total.astype(BF)
            for step in (1, 3, 2):
                second[h].append(
                    remote(
                        mid.at[h, (place[two] + step) % 4],
                        last.at[h, step - 1],
                        c_send.at[slot, 1, h, step - 1],
                        c_recv.at[slot, 1, h, step - 1],
                        dev(two, step),
                    )
                )
        hooks[1]()
        halves = []
        for h in range(2):
            one, two = order[h]
            for copy in second[h]:
                copy.wait_recv()
            total = mid[h, place[two]].astype(F32)
            for k in range(3):
                total = total + last[h, k].astype(F32)
            halves.append(total)
        return jnp.concatenate(halves, axis=1)

    out_weight = wout[...].reshape(HC, D)
    attended = scatter_sum(
        *rs1,
        lambda h: jnp.dot(
            context, out_weight[:, h * HALF : (h + 1) * HALF], preferred_element_type=F32
        ),
        "y",
        "z",
        1,
        (lambda: pass_weight("down0"), lambda: send_weight("down1")),
    )
    first_res = resid + modul(2) * attended
    normed_two = (layer_norm(first_res, 1e-05) * (1.0 + modul(4)) + modul(3)).astype(BF)
    order_two = (("x", "z"), ("z", "x"))
    bufs_two = (ag2a, ag2b)
    gather_own(
        bufs_two, ((normed_two[:, 0:HALF],), (normed_two[:, HALF:D],)), order_two
    )
    state = gather_first(bufs_two, order_two, 1)
    gather_second(bufs_two, order_two, 1, state)
    end_weight("up0")
    end_weight("up1")
    end_weight("down0")
    pass_weight("down1")
    gather_end(bufs_two, order_two, "z", state)
    tokens_two = rows32[...].astype(BF)
    have_weight("up0")
    have_weight("up1")
    inner = jax.nn.gelu(
        dot_nt(tokens_two, wup[...].reshape(SIDE * HID, D)), approximate=True
    ).astype(BF)
    end_weight("down1")
    have_weight("down0")
    have_weight("down1")
    down_weight = wdown[...].reshape(SIDE * HID, D)
    reduced = scatter_sum(
        *rs2,
        lambda h: jnp.dot(
            inner, down_weight[:, h * HALF : (h + 1) * HALF], preferred_element_type=F32
        ),
        "x",
        "z",
        3,
        (lambda: None, lambda: None),
    )
    near[2].wait()
    near[3].wait()
    second_res = first_res + modul(5) * reduced
    final = (
        layer_norm(second_res, 1e-05) * (1.0 + out_mod[1:2, :]) + out_mod[0:1, :]
    ).astype(BF)
    prediction = dot_nt(final, w_proj[...])
    swap[0:ROWS, 0:64] = prediction
    other = remote(
        swap.at[0:ROWS], swap.at[ROWS : 2 * ROWS], c_send.at[4, 1, 0, 0], c_recv.at[4, 1, 0, 0], sibling
    )
    other.wait_recv()
    theirs = swap[ROWS : 2 * ROWS, 0:64]
    is_cond = cfg == 0
    pred_cond = jnp.where(is_cond, prediction, theirs)
    pred_uncond = jnp.where(is_cond, theirs, prediction)
    guided = pred_uncond + guidance[0] * (pred_cond - pred_uncond)
    guided = jnp.where(is_cond, guided[:, 0:32], guided[:, 32:64])
    updated = solver[0] * latent[...] + solver[1] * guided
    keep = (row < counts[me]) & jnp.logical_not(is_text)
    out[...] = jnp.where(keep, updated, latent[...])
    for copy in sends:
        copy.wait_send()


def shards(
    hidden,
    latent,
    positions,
    counts,
    text_len,
    modulation,
    w_qkv,
    w_out,
    w_up,
    w_down,
    out_mod,
    w_proj,
    guidance,
    solver,
):
    vmem = pl.BlockSpec(memory_space=pltpu.VMEM)
    smem = pl.BlockSpec(memory_space=pltpu.SMEM)
    whole = pl.BlockSpec(memory_space=pl.ANY)

    def sums():
        return (
            pltpu.VMEM((2, SIDE, SIDE, ROWS, HALF), BF),
            pltpu.VMEM((2, 3, SIDE, ROWS, HALF), BF),
            pltpu.VMEM((2, SIDE, ROWS, HALF), BF),
            pltpu.VMEM((2, 3, ROWS, HALF), BF),
        )

    return pl.pallas_call(
        kernel,
        out_shape=jax.ShapeDtypeStruct(latent.shape, F32),
        in_specs=[vmem] * 3 + [smem] * 5 + [whole] * 8,
        out_specs=vmem,
        scratch_shapes=[
            pltpu.VMEM((ROWS, D), BF),
            pltpu.VMEM((6, 2, D), F32),
            pltpu.VMEM((2, D), F32),
            pltpu.VMEM((64, D), BF),
            pltpu.VMEM((3, SIDE, 48, D), BF),
            pltpu.VMEM((SIDE, 48, D), BF),
            pltpu.VMEM((SIDE, HID, D), BF),
            pltpu.VMEM((SIDE, HID, D), BF),
            pltpu.VMEM((SIDE, SIDE, ROWS, HALF + PAD), BF),
            pltpu.VMEM((SIDE, SIDE, ROWS, HALF), BF),
            pltpu.VMEM((SIDE, SIDE, ROWS, HALF), BF),
            pltpu.VMEM((SIDE, SIDE, ROWS, HALF), BF),
            pltpu.VMEM((SIDE * SIDE * ROWS, D), F32),
            pltpu.VMEM((SIDE, SIDE * SIDE * ROWS, 2 * HC), BF),
            sums(),
            sums(),
            pltpu.VMEM((SIDE * SIDE * ROWS, PAD), F32),
            pltpu.SemaphoreType.DMA((8, 4, 2)),
            pltpu.SemaphoreType.DMA((8, 4, 2)),
            pltpu.SemaphoreType.DMA((4,)),
            pltpu.SemaphoreType.DMA((8,)),
            pltpu.SemaphoreType.DMA((5, 2, 2, 3)),
            pltpu.SemaphoreType.DMA((5, 2, 2, 3)),
            pltpu.SemaphoreType.DMA((2, 2, 5, 3)),
            pltpu.SemaphoreType.DMA((2, 2, 5, 3)),
        ],
        compiler_params=pltpu.CompilerParams(
            collective_id=0, has_side_effects=True, vmem_limit_bytes=56 << 20
        ),
        name="step",
    )(
        latent,
        counts[None, :],
        jnp.asarray(frequencies()),
        positions.T,
        counts,
        text_len,
        guidance,
        solver,
        hidden[0],
        modulation.transpose(1, 0, 2),
        out_mod,
        w_proj.T,
        w_qkv.transpose(1, 2, 0),
        w_out,
        w_up.T,
        w_down,
    )


def solution(mesh):
    in_specs = (
        P("cfg", "seq", None),
        P("seq", "cfg"),
        P("seq", None),
        P(),
        P(),
        P(),
        P(None, None, "seq"),
        P("seq", None),
        P(None, "seq"),
        P("seq", None),
        P(),
        P(),
        P(),
        P(),
    )
    return jax.shard_map(
        shards, mesh=mesh, in_specs=in_specs, out_specs=P("seq", "cfg"), check_vma=False
    )
```

```python
import functools

import jax
import jax.numpy as jnp
import numpy as np
from jax import lax
from jax.experimental import pallas as pl
from jax.experimental.pallas import tpu as pltpu
from jax.sharding import PartitionSpec as P

D = 3072
HD = 64
SIDE = 4
ROWS = 8
HALF = D // 2
HC = 192
HID = 192
PAD = 128
BF = jnp.bfloat16
F32 = jnp.float32
NT = (((1,), (1,)), ((), ()))


def layer_norm(values, epsilon):
    center = values - jnp.mean(values, axis=-1, keepdims=True)
    spread = jnp.mean(center * center, axis=-1, keepdims=True)
    return center * lax.rsqrt(spread + epsilon)


def dot_nt(a, b):
    return lax.dot_general(a, b, NT, preferred_element_type=F32)


def exact_dot(a, b):
    return lax.dot_general(
        a,
        b,
        (((1,), (0,)), ((), ())),
        preferred_element_type=F32,
        precision=lax.Precision.HIGHEST,
    )


def frequencies():
    frame = 10000.0 ** (-2.0 * np.arange(8) / 16)
    side = 10000.0 ** (-2.0 * np.arange(12) / 24)
    pairs = np.concatenate([frame, side, side])
    return np.tile(np.repeat(pairs, 2), 3)[None, :].astype(np.float32)


def kernel(
    hidden_far,
    modulation_far,
    positions_far,
    text_len_far,
    counts_row_far,
    counts_far,
    freq_far,
    latent_far,
    guidance_far,
    solver_far,
    out_mod_far,
    w_proj_far,
    w_qkv,
    w_out,
    w_up,
    w_down,
    out,
    hidden,
    modulation,
    positions,
    text_len,
    counts_row,
    counts,
    freq,
    latent,
    guidance,
    solver,
    out_mod,
    w_proj,
    wqkv,
    wout,
    wup,
    wdown,
    ag1a,
    ag1b,
    ag2a,
    ag2b,
    rows32,
    kv,
    rs1,
    rs2,
    swap,
    w_send,
    w_recv,
    near_sem,
    local_sem,
    c_send,
    c_recv,
    g_send,
    g_recv,
):
    cfg = lax.axis_index("cfg")
    me = lax.axis_index("seq")
    z, y, x = me // 16, (me // 4) % 4, me % 4

    def dev(axis, step):
        zz = (z + step) % 4 if axis == "z" else z
        yy = (y + step) % 4 if axis == "y" else y
        xx = (x + step) % 4 if axis == "x" else x
        return (cfg, zz * 16 + yy * 4 + xx)

    place = {"x": x, "y": y, "z": z}
    sibling = (1 - cfg, me)
    sends = []

    def remote(src, dst, send, recv, device):
        copy = pltpu.make_async_remote_copy(
            src_ref=src,
            dst_ref=dst,
            send_sem=send,
            recv_sem=recv,
            device_id=device,
            device_id_type=pl.DeviceIdType.MESH,
        )
        copy.start()
        sends.append(copy)
        return copy

    barrier = pltpu.get_barrier_semaphore()
    everyone = [dev(axis, step) for axis in "xyz" for step in (1, 2, 3)] + [sibling]
    for device in everyone:
        pl.semaphore_signal(
            barrier, inc=1, device_id=device, device_id_type=pl.DeviceIdType.MESH
        )

    near = []
    for i, (far, ref) in enumerate(
        (
            (hidden_far, hidden),
            (modulation_far, modulation),
            (positions_far, positions),
            (text_len_far, text_len),
            (counts_row_far, counts_row),
            (counts_far, counts),
            (freq_far, freq),
            (latent_far, latent),
            (guidance_far, guidance),
            (solver_far, solver),
            (out_mod_far, out_mod),
            (w_proj_far, w_proj),
        )
    ):
        copy = pltpu.make_async_copy(far, ref, near_sem.at[i])
        copy.start()
        near.append(copy)

    top, bottom = pl.ds(0, HID // 2), pl.ds(HID // 2, HID // 2)
    weights = {
        "k": (0, w_qkv.at[1], lambda i: wqkv.at[1, i], "x"),
        "v": (1, w_qkv.at[2], lambda i: wqkv.at[2, i], "x"),
        "q": (2, w_qkv.at[0], lambda i: wqkv.at[0, i], "x"),
        "out": (3, w_out, lambda i: wout.at[i], "x"),
        "up0": (4, w_up.at[top], lambda i: wup.at[i, top], "y"),
        "up1": (5, w_up.at[bottom], lambda i: wup.at[i, bottom], "y"),
        "down0": (6, w_down.at[top], lambda i: wdown.at[i, top], "y"),
        "down1": (7, w_down.at[bottom], lambda i: wdown.at[i, bottom], "y"),
    }
    start = pl.multiple_of(cfg * HALF, HALF)
    half = pl.ds(start, HALF)
    quarters = (
        pl.ds(start, HALF // 2),
        pl.ds(pl.multiple_of(start + HALF // 2, HALF // 2), HALF // 2),
    )
    turns = (1, 3)
    moving = {}
    local = []

    def send_weight(name):
        slot, src, dst, axis = weights[name]
        moving[name, 0] = [
            remote(
                src.at[:, half],
                dst(place[axis]).at[:, half],
                w_send.at[slot, 0, i],
                w_recv.at[slot, 0, i],
                dev(axis, turn),
            )
            for i, turn in enumerate(turns)
        ]

    def pass_weight(name):
        slot, src, dst, axis = weights[name]
        moving[name, 1], moving[name, 2] = [], []
        for i, turn in enumerate(turns):
            moving[name, 0][i].wait_recv()
            block = dst((place[axis] - turn + 4) % 4)
            moving[name, 1].append(
                remote(
                    block.at[:, quarters[i]],
                    block.at[:, quarters[i]],
                    w_send.at[slot, 1, i],
                    w_recv.at[slot, 1, i],
                    dev(axis, turn),
                )
            )
            moving[name, 2].append(
                remote(
                    block.at[:, half],
                    block.at[:, half],
                    w_send.at[slot, 2, i],
                    w_recv.at[slot, 2, i],
                    sibling,
                )
            )

    def end_weight(name):
        slot, src, dst, axis = weights[name]
        for copy in moving[name, 1]:
            copy.wait_recv()
        block = dst((place[axis] + 2) % 4)
        moving[name, 2].append(
            remote(
                block.at[:, half],
                block.at[:, half],
                w_send.at[slot, 3, 0],
                w_recv.at[slot, 3, 0],
                sibling,
            )
        )

    def have_weight(name):
        for copy in moving[name, 2]:
            copy.wait_recv()
        local[weights[name][0]].wait()

    for copy in near[:4]:
        copy.wait()
    resid = hidden[...].astype(F32)
    row = lax.broadcasted_iota(jnp.int32, (ROWS, 1), 0)
    is_text = me * ROWS + row < text_len[0]

    def modul(k):
        two = modulation[k]
        return jnp.where(is_text, two[0:1, :], two[1:2, :])

    normed = (layer_norm(resid, 1e-05) * (1.0 + modul(1)) + modul(0)).astype(BF)

    def gather_own(bufs, values, orders):
        for buf, value, (p, q) in zip(bufs, values, orders):
            for i, part in enumerate(value):
                lo = 0 if i == 0 else HALF
                buf[place[q], place[p], :, lo : lo + part.shape[1]] = part

    def gather_first(bufs, orders, slot):
        first = []
        for h, (buf, (p, q)) in enumerate(zip(bufs, orders)):
            ref = buf.at[place[q], place[p]]
            first.append(
                [
                    remote(
                        ref,
                        ref,
                        g_send.at[slot, h, 0, step - 1],
                        g_recv.at[slot, h, 0, step - 1],
                        dev(p, step),
                    )
                    for step in (1, 3, 2)
                ]
            )
        return first, [gather_pass(bufs[h], orders[h], slot, h, 0) for h in range(2)]

    def gather_pass(buf, order, slot, h, behind):
        p, q = order
        ref = buf.at[place[q], (place[p] - behind + 4) % 4]
        return [
            remote(
                ref,
                ref,
                g_send.at[slot, h, behind + 1, step - 1],
                g_recv.at[slot, h, behind + 1, step - 1],
                dev(q, step),
            )
            for step in (1, 3, 2)
        ]

    def gather_second(bufs, orders, slot, state):
        first, second = state
        for i, behind in enumerate((1, 3, 2)):
            for h in range(2):
                first[h][i].wait_recv()
                second[h] += gather_pass(bufs[h], orders[h], slot, h, behind)

    def gather_end(bufs, orders, outer, state):
        for copy in state[1][0] + state[1][1]:
            copy.wait_recv()
        for h, (buf, (p, q)) in enumerate(zip(bufs, orders)):
            for i in range(SIDE):
                for j in range(SIDE):
                    at = (i * SIDE + j if q == outer else j * SIDE + i) * ROWS
                    rows32[at : at + ROWS, h * HALF : (h + 1) * HALF] = buf[
                        i, j, :, 0:HALF
                    ].astype(F32)

    lane = lax.broadcasted_iota(jnp.int32, (ROWS, PAD), 1)
    line = lax.broadcasted_iota(jnp.int32, (ROWS, PAD), 0)
    pos = jnp.zeros((ROWS, PAD), F32)
    for k in range(3):
        for r in range(ROWS):
            at = positions[k, r].astype(F32)
            pos = jnp.where((lane == k) & (line == r), at, pos)
    pos = jnp.where(is_text, 0.0, pos).astype(BF)
    order_one = (("y", "z"), ("y", "z"))
    bufs_one = (ag1a, ag1b)
    gather_own(
        bufs_one, ((normed[:, 0:HALF], pos), (normed[:, HALF:D],)), order_one
    )

    pl.semaphore_wait(barrier, len(everyone))

    state = gather_first(bufs_one, order_one, 0)
    for name in ("k", "v", "up0", "up1"):
        send_weight(name)
    for slot, src, dst, axis in weights.values():
        copy = pltpu.make_async_copy(src, dst(place[axis]), local_sem.at[slot])
        copy.start()
        local.append(copy)
    gather_second(bufs_one, order_one, 0, state)
    for copy in near[4:]:
        copy.wait()
    pass_weight("k")
    pass_weight("v")
    send_weight("q")
    send_weight("out")

    lane_a = lax.broadcasted_iota(jnp.int32, (HC, HC), 0)
    lane_b = lax.broadcasted_iota(jnp.int32, (HC, HC), 1)
    average = jnp.where(lane_a // HD == lane_b // HD, 1.0 / HD, 0.0).astype(F32)
    turn = (
        jnp.where((lane_a == lane_b + 1) & (lane_b % 2 == 0), -1.0, 0.0)
        + jnp.where((lane_a + 1 == lane_b) & (lane_b % 2 == 1), 1.0, 0.0)
    ).astype(F32)
    key = lax.broadcasted_iota(jnp.int32, (64, 512), 1)
    owner = (key // 32) % 4 * 16 + (key // 8) % 4 * 4 + key // 128
    pick = jnp.where(lax.broadcasted_iota(jnp.int32, (64, 512), 0) == owner, 1.0, 0.0)
    count_of = exact_dot(
        jnp.broadcast_to(counts_row[...].astype(F32), (ROWS, 64)), pick.astype(F32)
    )
    key_row = lax.broadcasted_iota(jnp.int32, (ROWS, 512), 1) % ROWS
    live = jnp.where(key_row.astype(F32) < count_of, 1.0, 0.0)[0:1, :]
    dim = lax.broadcasted_iota(jnp.int32, (PAD, HC), 1) % HD
    which = jnp.where(dim < 16, 0, jnp.where(dim < 40, 1, 2))
    axis_of = jnp.where(
        lax.broadcasted_iota(jnp.int32, (PAD, HC), 0) == which, 1.0, 0.0
    ).astype(F32)

    end_weight("k")
    end_weight("v")
    pass_weight("up0")
    send_weight("down0")
    pass_weight("q")
    gather_end(bufs_one, order_one, "z", state)
    for z_at in range(SIDE):
        for y_at in range(SIDE):
            at = (z_at * SIDE + y_at) * ROWS
            swap[at : at + ROWS, :] = ag1a[z_at, y_at, :, HALF : HALF + PAD].astype(F32)
    angles = exact_dot(swap[...], axis_of) * freq[...]
    cosine = jnp.cos(angles)
    sine = jnp.sin(angles)
    tokens = rows32[...].astype(BF)

    pass_weight("up1")

    def heads(columns):
        values = columns.astype(BF).astype(F32)
        center = values - exact_dot(values, average)
        spread = exact_dot(center * center, average)
        unit = center * lax.rsqrt(spread + 1e-06)
        return unit * cosine + exact_dot(unit, turn) * sine

    def project(part):
        return dot_nt(tokens, wqkv[part].reshape(HC, D))

    have_weight("k")
    keys = heads(project(1)).astype(BF)
    have_weight("v")
    kv[x, :, 0:HC] = keys
    kv[x, :, HC : 2 * HC] = project(2).astype(BF)
    moved = [
        remote(
            kv.at[x],
            kv.at[x],
            c_send.at[4, 0, 0, step - 1],
            c_recv.at[4, 0, 0, step - 1],
            dev("x", step),
        )
        for step in (1, 3, 2)
    ]
    end_weight("q")
    pass_weight("out")
    have_weight("q")
    queries = (heads(project(0)) * HD ** (-0.5)).astype(BF)
    for copy in moved:
        copy.wait_recv()
    end_weight("out")

    all_keys = kv[:, :, 0:HC].reshape(4 * 128, HC)
    all_values = kv[:, :, 128 : 2 * HC].reshape(4 * 128, 2 * HC - 128)
    lane_q = lax.broadcasted_iota(jnp.int32, (1, HC), 1) // HD
    lane_v = lax.broadcasted_iota(jnp.int32, (1, 256), 1) // HD - 1
    context = jnp.zeros((128, 256), F32)
    for head in range(HC // HD):
        chosen = jnp.where(lane_q == head, queries, jnp.zeros_like(queries))
        attend = jnp.exp(dot_nt(chosen, all_keys)) * live
        denom = jnp.sum(attend, axis=1, keepdims=True)
        numer = jnp.dot(attend.astype(BF), all_values, preferred_element_type=F32)
        context = jnp.where(lane_v == head, numer / denom, context)
    context = context[:, 64:256].astype(BF)
    have_weight("out")

    def scatter_sum(send, recv, mid, last, produce, p, q, slot, hooks):
        order = ((q, p), (p, q))
        copies = [[], []]
        for h in range(2):
            part = produce(h)
            for q_at in range(SIDE):
                for p_at in range(SIDE):
                    at = (q_at * SIDE + p_at) * ROWS
                    i, j = (q_at, p_at) if h == 0 else (p_at, q_at)
                    send[h, i, j] = part[at : at + ROWS, :].astype(BF)
            for step in (1, 3, 2):
                one = order[h][0]
                copies[h].append(
                    remote(
                        send.at[h, (place[one] + step) % 4],
                        recv.at[h, step - 1],
                        c_send.at[slot, 0, h, step - 1],
                        c_recv.at[slot, 0, h, step - 1],
                        dev(one, step),
                    )
                )
        hooks[0]()
        second = [[], []]
        for h in range(2):
            one, two = order[h]
            for copy in copies[h]:
                copy.wait_recv()
            for j in range(SIDE):
                total = send[h, place[one], j].astype(F32)
                for k in range(3):
                    total = total + recv[h, k, j].astype(F32)
                mid[h, j] = total.astype(BF)
            for step in (1, 3, 2):
                second[h].append(
                    remote(
                        mid.at[h, (place[two] + step) % 4],
                        last.at[h, step - 1],
                        c_send.at[slot, 1, h, step - 1],
                        c_recv.at[slot, 1, h, step - 1],
                        dev(two, step),
                    )
                )
        hooks[1]()
        halves = []
        for h in range(2):
            one, two = order[h]
            for copy in second[h]:
                copy.wait_recv()
            total = mid[h, place[two]].astype(F32)
            for k in range(3):
                total = total + last[h, k].astype(F32)
            halves.append(total)
        return jnp.concatenate(halves, axis=1)

    out_weight = wout[...].reshape(HC, D)
    attended = scatter_sum(
        *rs1,
        lambda h: jnp.dot(
            context, out_weight[:, h * HALF : (h + 1) * HALF], preferred_element_type=F32
        ),
        "y",
        "z",
        1,
        (lambda: pass_weight("down0"), lambda: send_weight("down1")),
    )
    first_res = resid + modul(2) * attended
    normed_two = (layer_norm(first_res, 1e-05) * (1.0 + modul(4)) + modul(3)).astype(BF)
    order_two = (("x", "z"), ("z", "x"))
    bufs_two = (ag2a, ag2b)
    gather_own(
        bufs_two, ((normed_two[:, 0:HALF],), (normed_two[:, HALF:D],)), order_two
    )
    state = gather_first(bufs_two, order_two, 1)
    gather_second(bufs_two, order_two, 1, state)
    end_weight("up0")
    end_weight("up1")
    end_weight("down0")
    pass_weight("down1")
    gather_end(bufs_two, order_two, "z", state)
    tokens_two = rows32[...].astype(BF)
    have_weight("up0")
    have_weight("up1")
    inner = jax.nn.gelu(
        dot_nt(tokens_two, wup[...].reshape(SIDE * HID, D)), approximate=True
    ).astype(BF)
    end_weight("down1")
    have_weight("down0")
    have_weight("down1")
    down_weight = wdown[...].reshape(SIDE * HID, D)
    reduced = scatter_sum(
        *rs2,
        lambda h: jnp.dot(
            inner, down_weight[:, h * HALF : (h + 1) * HALF], preferred_element_type=F32
        ),
        "x",
        "z",
        3,
        (lambda: None, lambda: None),
    )
    second_res = first_res + modul(5) * reduced
    final = (
        layer_norm(second_res, 1e-05) * (1.0 + out_mod[1:2, :]) + out_mod[0:1, :]
    ).astype(BF)
    prediction = dot_nt(final, w_proj[...])
    swap[0:ROWS, 0:64] = prediction
    other = remote(
        swap.at[0:ROWS], swap.at[ROWS : 2 * ROWS], c_send.at[4, 1, 0, 0], c_recv.at[4, 1, 0, 0], sibling
    )
    other.wait_recv()
    theirs = swap[ROWS : 2 * ROWS, 0:64]
    is_cond = cfg == 0
    pred_cond = jnp.where(is_cond, prediction, theirs)
    pred_uncond = jnp.where(is_cond, theirs, prediction)
    guided = pred_uncond + guidance[0] * (pred_cond - pred_uncond)
    guided = jnp.where(is_cond, guided[:, 0:32], guided[:, 32:64])
    updated = solver[0] * latent[...] + solver[1] * guided
    keep = (row < counts[me]) & jnp.logical_not(is_text)
    out[...] = jnp.where(keep, updated, latent[...])
    for copy in sends:
        copy.wait_send()


def shards(
    hidden,
    latent,
    positions,
    counts,
    text_len,
    modulation,
    w_qkv,
    w_out,
    w_up,
    w_down,
    out_mod,
    w_proj,
    guidance,
    solver,
):
    vmem = pl.BlockSpec(memory_space=pltpu.VMEM)
    whole = pl.BlockSpec(memory_space=pl.ANY)

    def sums():
        return (
            pltpu.VMEM((2, SIDE, SIDE, ROWS, HALF), BF),
            pltpu.VMEM((2, 3, SIDE, ROWS, HALF), BF),
            pltpu.VMEM((2, SIDE, ROWS, HALF), BF),
            pltpu.VMEM((2, 3, ROWS, HALF), BF),
        )

    return pl.pallas_call(
        kernel,
        out_shape=jax.ShapeDtypeStruct(latent.shape, F32),
        in_specs=[whole] * 16,
        out_specs=vmem,
        scratch_shapes=[
            pltpu.VMEM((ROWS, D), BF),
            pltpu.VMEM((6, 2, D), F32),
            pltpu.SMEM((3, ROWS), jnp.int32),
            pltpu.SMEM((1,), jnp.int32),
            pltpu.VMEM((1, 64), jnp.int32),
            pltpu.SMEM((64,), jnp.int32),
            pltpu.VMEM((1, HC), F32),
            pltpu.VMEM((ROWS, 32), F32),
            pltpu.SMEM((1,), F32),
            pltpu.SMEM((2,), F32),
            pltpu.VMEM((2, D), F32),
            pltpu.VMEM((64, D), BF),
            pltpu.VMEM((3, SIDE, 48, D), BF),
            pltpu.VMEM((SIDE, 48, D), BF),
            pltpu.VMEM((SIDE, HID, D), BF),
            pltpu.VMEM((SIDE, HID, D), BF),
            pltpu.VMEM((SIDE, SIDE, ROWS, HALF + PAD), BF),
            pltpu.VMEM((SIDE, SIDE, ROWS, HALF), BF),
            pltpu.VMEM((SIDE, SIDE, ROWS, HALF), BF),
            pltpu.VMEM((SIDE, SIDE, ROWS, HALF), BF),
            pltpu.VMEM((SIDE * SIDE * ROWS, D), F32),
            pltpu.VMEM((SIDE, SIDE * SIDE * ROWS, 2 * HC), BF),
            sums(),
            sums(),
            pltpu.VMEM((SIDE * SIDE * ROWS, PAD), F32),
            pltpu.SemaphoreType.DMA((8, 4, 2)),
            pltpu.SemaphoreType.DMA((8, 4, 2)),
            pltpu.SemaphoreType.DMA((12,)),
            pltpu.SemaphoreType.DMA((8,)),
            pltpu.SemaphoreType.DMA((5, 2, 2, 3)),
            pltpu.SemaphoreType.DMA((5, 2, 2, 3)),
            pltpu.SemaphoreType.DMA((2, 2, 5, 3)),
            pltpu.SemaphoreType.DMA((2, 2, 5, 3)),
        ],
        compiler_params=pltpu.CompilerParams(
            collective_id=0, has_side_effects=True, vmem_limit_bytes=56 << 20
        ),
        name="step",
    )(
        hidden[0],
        modulation.transpose(1, 0, 2),
        positions.T,
        text_len,
        counts[None, :],
        counts,
        jnp.asarray(frequencies()),
        latent,
        guidance,
        solver,
        out_mod,
        w_proj.T,
        w_qkv.transpose(1, 2, 0),
        w_out,
        w_up.T,
        w_down,
    )


def solution(mesh):
    in_specs = (
        P("cfg", "seq", None),
        P("seq", "cfg"),
        P("seq", None),
        P(),
        P(),
        P(),
        P(None, None, "seq"),
        P("seq", None),
        P(None, "seq"),
        P("seq", None),
        P(),
        P(),
        P(),
        P(),
    )
    return jax.shard_map(
        shards, mesh=mesh, in_specs=in_specs, out_specs=P("seq", "cfg"), check_vma=False
    )
```

```python
import functools

import jax
import jax.numpy as jnp
import numpy as np
from jax import lax
from jax.experimental import pallas as pl
from jax.experimental.pallas import tpu as pltpu
from jax.sharding import PartitionSpec as P

D = 3072
HD = 64
SIDE = 4
ROWS = 8
HALF = D // 2
HC = 192
HID = 192
PAD = 128
BF = jnp.bfloat16
F32 = jnp.float32
NT = (((1,), (1,)), ((), ()))


def layer_norm(values, epsilon):
    center = values - jnp.mean(values, axis=-1, keepdims=True)
    spread = jnp.mean(center * center, axis=-1, keepdims=True)
    return center * lax.rsqrt(spread + epsilon)


def dot_nt(a, b):
    return lax.dot_general(a, b, NT, preferred_element_type=F32)


def exact_dot(a, b):
    return lax.dot_general(
        a,
        b,
        (((1,), (0,)), ((), ())),
        preferred_element_type=F32,
        precision=lax.Precision.HIGHEST,
    )


def frequencies():
    frame = 10000.0 ** (-2.0 * np.arange(8) / 16)
    side = 10000.0 ** (-2.0 * np.arange(12) / 24)
    pairs = np.concatenate([frame, side, side])
    return np.tile(np.repeat(pairs, 2), 3)[None, :].astype(np.float32)


def kernel(
    hidden_far,
    modulation_far,
    positions_far,
    text_len_far,
    counts_row_far,
    counts_far,
    freq_far,
    latent_far,
    guidance_far,
    solver_far,
    out_mod_far,
    w_proj_far,
    w_qkv,
    w_out,
    w_up,
    w_down,
    out,
    hidden,
    modulation,
    positions,
    text_len,
    counts_row,
    counts,
    freq,
    latent,
    guidance,
    solver,
    out_mod,
    w_proj,
    wqkv,
    wout,
    wup,
    wdown,
    ag1a,
    ag1b,
    ag2a,
    ag2b,
    rows32,
    kv,
    rs1,
    rs2,
    swap,
    w_send,
    w_recv,
    near_sem,
    local_sem,
    c_send,
    c_recv,
    g_send,
    g_recv,
):
    cfg = lax.axis_index("cfg")
    me = lax.axis_index("seq")
    z, y, x = me // 16, (me // 4) % 4, me % 4

    def dev(axis, step):
        zz = (z + step) % 4 if axis == "z" else z
        yy = (y + step) % 4 if axis == "y" else y
        xx = (x + step) % 4 if axis == "x" else x
        return (cfg, zz * 16 + yy * 4 + xx)

    place = {"x": x, "y": y, "z": z}
    sibling = (1 - cfg, me)
    sends = []

    def remote(src, dst, send, recv, device):
        copy = pltpu.make_async_remote_copy(
            src_ref=src,
            dst_ref=dst,
            send_sem=send,
            recv_sem=recv,
            device_id=device,
            device_id_type=pl.DeviceIdType.MESH,
        )
        copy.start()
        sends.append(copy)
        return copy

    barrier = pltpu.get_barrier_semaphore()
    everyone = [dev(axis, step) for axis in "xyz" for step in (1, 2, 3)] + [sibling]
    for device in everyone:
        pl.semaphore_signal(
            barrier, inc=1, device_id=device, device_id_type=pl.DeviceIdType.MESH
        )

    near = []
    for i, (far, ref) in enumerate(
        (
            (hidden_far, hidden),
            (modulation_far, modulation),
            (positions_far, positions),
            (text_len_far, text_len),
            (counts_row_far, counts_row),
            (counts_far, counts),
            (freq_far, freq),
            (latent_far, latent),
            (guidance_far, guidance),
            (solver_far, solver),
            (out_mod_far, out_mod),
            (w_proj_far, w_proj),
        )
    ):
        copy = pltpu.make_async_copy(far, ref, near_sem.at[i])
        copy.start()
        near.append(copy)

    top, bottom = pl.ds(0, HID // 2), pl.ds(HID // 2, HID // 2)
    weights = {
        "k": (0, w_qkv.at[1], lambda i: wqkv.at[1, i], "x"),
        "v": (1, w_qkv.at[2], lambda i: wqkv.at[2, i], "x"),
        "q": (2, w_qkv.at[0], lambda i: wqkv.at[0, i], "x"),
        "out": (3, w_out, lambda i: wout.at[i], "x"),
        "up0": (4, w_up.at[top], lambda i: wup.at[i, top], "y"),
        "up1": (5, w_up.at[bottom], lambda i: wup.at[i, bottom], "y"),
        "down0": (6, w_down.at[top], lambda i: wdown.at[i, top], "y"),
        "down1": (7, w_down.at[bottom], lambda i: wdown.at[i, bottom], "y"),
    }
    start = pl.multiple_of(cfg * HALF, HALF)
    half = pl.ds(start, HALF)
    quarters = (
        pl.ds(start, HALF // 2),
        pl.ds(pl.multiple_of(start + HALF // 2, HALF // 2), HALF // 2),
    )
    turns = (1, 3)
    moving = {}
    local = []

    def send_weight(name):
        slot, src, dst, axis = weights[name]
        moving[name, 0] = [
            remote(
                src.at[:, half],
                dst(place[axis]).at[:, half],
                w_send.at[slot, 0, i],
                w_recv.at[slot, 0, i],
                dev(axis, turn),
            )
            for i, turn in enumerate(turns)
        ]

    def pass_weight(name):
        slot, src, dst, axis = weights[name]
        moving[name, 1], moving[name, 2] = [], []
        for i, turn in enumerate(turns):
            moving[name, 0][i].wait_recv()
            block = dst((place[axis] - turn + 4) % 4)
            moving[name, 1].append(
                remote(
                    block.at[:, quarters[i]],
                    block.at[:, quarters[i]],
                    w_send.at[slot, 1, i],
                    w_recv.at[slot, 1, i],
                    dev(axis, turn),
                )
            )
            moving[name, 2].append(
                remote(
                    block.at[:, half],
                    block.at[:, half],
                    w_send.at[slot, 2, i],
                    w_recv.at[slot, 2, i],
                    sibling,
                )
            )

    def end_weight(name):
        slot, src, dst, axis = weights[name]
        for copy in moving[name, 1]:
            copy.wait_recv()
        block = dst((place[axis] + 2) % 4)
        moving[name, 2].append(
            remote(
                block.at[:, half],
                block.at[:, half],
                w_send.at[slot, 3, 0],
                w_recv.at[slot, 3, 0],
                sibling,
            )
        )

    def have_weight(name):
        for copy in moving[name, 2]:
            copy.wait_recv()
        local[weights[name][0]].wait()

    for copy in near[:4]:
        copy.wait()
    resid = hidden[...].astype(F32)
    row = lax.broadcasted_iota(jnp.int32, (ROWS, 1), 0)
    is_text = me * ROWS + row < text_len[0]

    def modul(k):
        two = modulation[k]
        return jnp.where(is_text, two[0:1, :], two[1:2, :])

    normed = (layer_norm(resid, 1e-05) * (1.0 + modul(1)) + modul(0)).astype(BF)

    def gather_own(bufs, values, orders):
        for buf, value, (p, q) in zip(bufs, values, orders):
            for i, part in enumerate(value):
                lo = 0 if i == 0 else HALF
                buf[place[q], place[p], :, lo : lo + part.shape[1]] = part

    def gather_first(bufs, orders, slot):
        first = []
        for h, (buf, (p, q)) in enumerate(zip(bufs, orders)):
            ref = buf.at[place[q], place[p]]
            first.append(
                [
                    remote(
                        ref,
                        ref,
                        g_send.at[slot, h, 0, step - 1],
                        g_recv.at[slot, h, 0, step - 1],
                        dev(p, step),
                    )
                    for step in (1, 3, 2)
                ]
            )
        return first, [gather_pass(bufs[h], orders[h], slot, h, 0) for h in range(2)]

    def gather_pass(buf, order, slot, h, behind):
        p, q = order
        ref = buf.at[place[q], (place[p] - behind + 4) % 4]
        return [
            remote(
                ref,
                ref,
                g_send.at[slot, h, behind + 1, step - 1],
                g_recv.at[slot, h, behind + 1, step - 1],
                dev(q, step),
            )
            for step in (2, 1, 3)
        ]

    def gather_second(bufs, orders, slot, state):
        first, second = state
        for i, behind in enumerate((1, 3, 2)):
            for h in range(2):
                first[h][i].wait_recv()
                second[h] += gather_pass(bufs[h], orders[h], slot, h, behind)

    def gather_end(bufs, orders, outer, state):
        for copy in state[1][0] + state[1][1]:
            copy.wait_recv()
        for h, (buf, (p, q)) in enumerate(zip(bufs, orders)):
            for i in range(SIDE):
                for j in range(SIDE):
                    at = (i * SIDE + j if q == outer else j * SIDE + i) * ROWS
                    rows32[at : at + ROWS, h * HALF : (h + 1) * HALF] = buf[
                        i, j, :, 0:HALF
                    ].astype(F32)

    lane = lax.broadcasted_iota(jnp.int32, (ROWS, PAD), 1)
    line = lax.broadcasted_iota(jnp.int32, (ROWS, PAD), 0)
    pos = jnp.zeros((ROWS, PAD), F32)
    for k in range(3):
        for r in range(ROWS):
            at = positions[k, r].astype(F32)
            pos = jnp.where((lane == k) & (line == r), at, pos)
    pos = jnp.where(is_text, 0.0, pos).astype(BF)
    order_one = (("y", "z"), ("y", "z"))
    bufs_one = (ag1a, ag1b)
    gather_own(
        bufs_one, ((normed[:, 0:HALF], pos), (normed[:, HALF:D],)), order_one
    )

    pl.semaphore_wait(barrier, len(everyone))

    state = gather_first(bufs_one, order_one, 0)
    for name in ("k", "v", "up0", "up1"):
        send_weight(name)
    for slot, src, dst, axis in weights.values():
        copy = pltpu.make_async_copy(src, dst(place[axis]), local_sem.at[slot])
        copy.start()
        local.append(copy)
    gather_second(bufs_one, order_one, 0, state)
    for copy in near[4:]:
        copy.wait()
    pass_weight("k")
    pass_weight("v")
    send_weight("q")
    send_weight("out")

    lane_a = lax.broadcasted_iota(jnp.int32, (HC, HC), 0)
    lane_b = lax.broadcasted_iota(jnp.int32, (HC, HC), 1)
    average = jnp.where(lane_a // HD == lane_b // HD, 1.0 / HD, 0.0).astype(F32)
    turn = (
        jnp.where((lane_a == lane_b + 1) & (lane_b % 2 == 0), -1.0, 0.0)
        + jnp.where((lane_a + 1 == lane_b) & (lane_b % 2 == 1), 1.0, 0.0)
    ).astype(F32)
    key = lax.broadcasted_iota(jnp.int32, (64, 512), 1)
    owner = (key // 32) % 4 * 16 + (key // 8) % 4 * 4 + key // 128
    pick = jnp.where(lax.broadcasted_iota(jnp.int32, (64, 512), 0) == owner, 1.0, 0.0)
    count_of = exact_dot(
        jnp.broadcast_to(counts_row[...].astype(F32), (ROWS, 64)), pick.astype(F32)
    )
    key_row = lax.broadcasted_iota(jnp.int32, (ROWS, 512), 1) % ROWS
    live = jnp.where(key_row.astype(F32) < count_of, 1.0, 0.0)[0:1, :]
    dim = lax.broadcasted_iota(jnp.int32, (PAD, HC), 1) % HD
    which = jnp.where(dim < 16, 0, jnp.where(dim < 40, 1, 2))
    axis_of = jnp.where(
        lax.broadcasted_iota(jnp.int32, (PAD, HC), 0) == which, 1.0, 0.0
    ).astype(F32)

    end_weight("k")
    end_weight("v")
    pass_weight("up0")
    send_weight("down0")
    gather_end(bufs_one, order_one, "z", state)
    for z_at in range(SIDE):
        for y_at in range(SIDE):
            at = (z_at * SIDE + y_at) * ROWS
            swap[at : at + ROWS, :] = ag1a[z_at, y_at, :, HALF : HALF + PAD].astype(F32)
    angles = exact_dot(swap[...], axis_of) * freq[...]
    cosine = jnp.cos(angles)
    sine = jnp.sin(angles)
    tokens = rows32[...].astype(BF)

    def heads(columns):
        values = columns.astype(BF).astype(F32)
        center = values - exact_dot(values, average)
        spread = exact_dot(center * center, average)
        unit = center * lax.rsqrt(spread + 1e-06)
        return unit * cosine + exact_dot(unit, turn) * sine

    def project(part):
        return dot_nt(tokens, wqkv[part].reshape(HC, D))

    pass_weight("q")
    have_weight("k")
    keys = heads(project(1)).astype(BF)
    have_weight("v")
    kv[x, :, 0:HC] = keys
    kv[x, :, HC : 2 * HC] = project(2).astype(BF)
    moved = [
        remote(
            kv.at[x],
            kv.at[x],
            c_send.at[4, 0, 0, step - 1],
            c_recv.at[4, 0, 0, step - 1],
            dev("x", step),
        )
        for step in (2, 1, 3)
    ]
    end_weight("q")
    pass_weight("out")
    pass_weight("up1")
    have_weight("q")
    queries = (heads(project(0)) * HD ** (-0.5)).astype(BF)
    for copy in moved:
        copy.wait_recv()
    end_weight("out")

    all_keys = kv[:, :, 0:HC].reshape(4 * 128, HC)
    all_values = kv[:, :, 128 : 2 * HC].reshape(4 * 128, 2 * HC - 128)
    lane_q = lax.broadcasted_iota(jnp.int32, (1, HC), 1) // HD
    lane_v = lax.broadcasted_iota(jnp.int32, (1, 256), 1) // HD - 1
    context = jnp.zeros((128, 256), F32)
    for head in range(HC // HD):
        chosen = jnp.where(lane_q == head, queries, jnp.zeros_like(queries))
        attend = jnp.exp(dot_nt(chosen, all_keys)) * live
        denom = jnp.sum(attend, axis=1, keepdims=True)
        numer = jnp.dot(attend.astype(BF), all_values, preferred_element_type=F32)
        context = jnp.where(lane_v == head, numer / denom, context)
    context = context[:, 64:256].astype(BF)
    have_weight("out")

    def scatter_sum(send, recv, mid, last, produce, p, q, slot, hooks):
        order = ((q, p), (p, q))
        copies = [[], []]
        for h in range(2):
            part = produce(h)
            for q_at in range(SIDE):
                for p_at in range(SIDE):
                    at = (q_at * SIDE + p_at) * ROWS
                    i, j = (q_at, p_at) if h == 0 else (p_at, q_at)
                    send[h, i, j] = part[at : at + ROWS, :].astype(BF)
            for step in (2, 1, 3):
                one = order[h][0]
                copies[h].append(
                    remote(
                        send.at[h, (place[one] + step) % 4],
                        recv.at[h, step - 1],
                        c_send.at[slot, 0, h, step - 1],
                        c_recv.at[slot, 0, h, step - 1],
                        dev(one, step),
                    )
                )
        hooks[0]()
        second = [[], []]
        for h in range(2):
            one, two = order[h]
            for copy in copies[h]:
                copy.wait_recv()
            for j in range(SIDE):
                total = send[h, place[one], j].astype(F32)
                for k in range(3):
                    total = total + recv[h, k, j].astype(F32)
                mid[h, j] = total.astype(BF)
            for step in (2, 1, 3):
                second[h].append(
                    remote(
                        mid.at[h, (place[two] + step) % 4],
                        last.at[h, step - 1],
                        c_send.at[slot, 1, h, step - 1],
                        c_recv.at[slot, 1, h, step - 1],
                        dev(two, step),
                    )
                )
        hooks[1]()
        halves = []
        for h in range(2):
            one, two = order[h]
            for copy in second[h]:
                copy.wait_recv()
            total = mid[h, place[two]].astype(F32)
            for k in range(3):
                total = total + last[h, k].astype(F32)
            halves.append(total)
        return jnp.concatenate(halves, axis=1)

    out_weight = wout[...].reshape(HC, D)
    attended = scatter_sum(
        *rs1,
        lambda h: jnp.dot(
            context, out_weight[:, h * HALF : (h + 1) * HALF], preferred_element_type=F32
        ),
        "y",
        "z",
        1,
        (lambda: pass_weight("down0"), lambda: send_weight("down1")),
    )
    first_res = resid + modul(2) * attended
    normed_two = (layer_norm(first_res, 1e-05) * (1.0 + modul(4)) + modul(3)).astype(BF)
    order_two = (("x", "z"), ("z", "x"))
    bufs_two = (ag2a, ag2b)
    gather_own(
        bufs_two, ((normed_two[:, 0:HALF],), (normed_two[:, HALF:D],)), order_two
    )
    state = gather_first(bufs_two, order_two, 1)
    gather_second(bufs_two, order_two, 1, state)
    end_weight("up0")
    end_weight("up1")
    end_weight("down0")
    pass_weight("down1")
    gather_end(bufs_two, order_two, "z", state)
    tokens_two = rows32[...].astype(BF)
    have_weight("up0")
    have_weight("up1")
    inner = jax.nn.gelu(
        dot_nt(tokens_two, wup[...].reshape(SIDE * HID, D)), approximate=True
    ).astype(BF)
    end_weight("down1")
    have_weight("down0")
    have_weight("down1")
    down_weight = wdown[...].reshape(SIDE * HID, D)
    reduced = scatter_sum(
        *rs2,
        lambda h: jnp.dot(
            inner, down_weight[:, h * HALF : (h + 1) * HALF], preferred_element_type=F32
        ),
        "x",
        "z",
        3,
        (lambda: None, lambda: None),
    )
    second_res = first_res + modul(5) * reduced
    final = (
        layer_norm(second_res, 1e-05) * (1.0 + out_mod[1:2, :]) + out_mod[0:1, :]
    ).astype(BF)
    prediction = dot_nt(final, w_proj[...])
    swap[0:ROWS, 0:64] = prediction
    other = remote(
        swap.at[0:ROWS], swap.at[ROWS : 2 * ROWS], c_send.at[4, 1, 0, 0], c_recv.at[4, 1, 0, 0], sibling
    )
    other.wait_recv()
    theirs = swap[ROWS : 2 * ROWS, 0:64]
    is_cond = cfg == 0
    pred_cond = jnp.where(is_cond, prediction, theirs)
    pred_uncond = jnp.where(is_cond, theirs, prediction)
    guided = pred_uncond + guidance[0] * (pred_cond - pred_uncond)
    guided = jnp.where(is_cond, guided[:, 0:32], guided[:, 32:64])
    updated = solver[0] * latent[...] + solver[1] * guided
    keep = (row < counts[me]) & jnp.logical_not(is_text)
    out[...] = jnp.where(keep, updated, latent[...])
    for copy in sends:
        copy.wait_send()


def shards(
    hidden,
    latent,
    positions,
    counts,
    text_len,
    modulation,
    w_qkv,
    w_out,
    w_up,
    w_down,
    out_mod,
    w_proj,
    guidance,
    solver,
):
    vmem = pl.BlockSpec(memory_space=pltpu.VMEM)
    whole = pl.BlockSpec(memory_space=pl.ANY)

    def sums():
        return (
            pltpu.VMEM((2, SIDE, SIDE, ROWS, HALF), BF),
            pltpu.VMEM((2, 3, SIDE, ROWS, HALF), BF),
            pltpu.VMEM((2, SIDE, ROWS, HALF), BF),
            pltpu.VMEM((2, 3, ROWS, HALF), BF),
        )

    return pl.pallas_call(
        kernel,
        out_shape=jax.ShapeDtypeStruct(latent.shape, F32),
        in_specs=[whole] * 16,
        out_specs=vmem,
        scratch_shapes=[
            pltpu.VMEM((ROWS, D), BF),
            pltpu.VMEM((6, 2, D), F32),
            pltpu.SMEM((3, ROWS), jnp.int32),
            pltpu.SMEM((1,), jnp.int32),
            pltpu.VMEM((1, 64), jnp.int32),
            pltpu.SMEM((64,), jnp.int32),
            pltpu.VMEM((1, HC), F32),
            pltpu.VMEM((ROWS, 32), F32),
            pltpu.SMEM((1,), F32),
            pltpu.SMEM((2,), F32),
            pltpu.VMEM((2, D), F32),
            pltpu.VMEM((64, D), BF),
            pltpu.VMEM((3, SIDE, 48, D), BF),
            pltpu.VMEM((SIDE, 48, D), BF),
            pltpu.VMEM((SIDE, HID, D), BF),
            pltpu.VMEM((SIDE, HID, D), BF),
            pltpu.VMEM((SIDE, SIDE, ROWS, HALF + PAD), BF),
            pltpu.VMEM((SIDE, SIDE, ROWS, HALF), BF),
            pltpu.VMEM((SIDE, SIDE, ROWS, HALF), BF),
            pltpu.VMEM((SIDE, SIDE, ROWS, HALF), BF),
            pltpu.VMEM((SIDE * SIDE * ROWS, D), F32),
            pltpu.VMEM((SIDE, SIDE * SIDE * ROWS, 2 * HC), BF),
            sums(),
            sums(),
            pltpu.VMEM((SIDE * SIDE * ROWS, PAD), F32),
            pltpu.SemaphoreType.DMA((8, 4, 2)),
            pltpu.SemaphoreType.DMA((8, 4, 2)),
            pltpu.SemaphoreType.DMA((12,)),
            pltpu.SemaphoreType.DMA((8,)),
            pltpu.SemaphoreType.DMA((5, 2, 2, 3)),
            pltpu.SemaphoreType.DMA((5, 2, 2, 3)),
            pltpu.SemaphoreType.DMA((2, 2, 5, 3)),
            pltpu.SemaphoreType.DMA((2, 2, 5, 3)),
        ],
        compiler_params=pltpu.CompilerParams(
            collective_id=0, has_side_effects=True, vmem_limit_bytes=56 << 20
        ),
        name="step",
    )(
        hidden[0],
        modulation.transpose(1, 0, 2),
        positions.T,
        text_len,
        counts[None, :],
        counts,
        jnp.asarray(frequencies()),
        latent,
        guidance,
        solver,
        out_mod,
        w_proj.T,
        w_qkv.transpose(1, 2, 0),
        w_out,
        w_up.T,
        w_down,
    )


def solution(mesh):
    in_specs = (
        P("cfg", "seq", None),
        P("seq", "cfg"),
        P("seq", None),
        P(),
        P(),
        P(),
        P(None, None, "seq"),
        P("seq", None),
        P(None, "seq"),
        P("seq", None),
        P(),
        P(),
        P(),
        P(),
    )
    return jax.shard_map(
        shards, mesh=mesh, in_specs=in_specs, out_specs=P("seq", "cfg"), check_vma=False
    )
```

```python
import functools

import jax
import jax.numpy as jnp
import numpy as np
from jax import lax
from jax.experimental import pallas as pl
from jax.experimental.pallas import tpu as pltpu
from jax.sharding import PartitionSpec as P

D = 3072
HD = 64
SIDE = 4
ROWS = 8
HALF = D // 2
HC = 192
HID = 192
PAD = 128
BF = jnp.bfloat16
F32 = jnp.float32
NT = (((1,), (1,)), ((), ()))


def layer_norm(values, epsilon):
    center = values - jnp.mean(values, axis=-1, keepdims=True)
    spread = jnp.mean(center * center, axis=-1, keepdims=True)
    return center * lax.rsqrt(spread + epsilon)


def dot_nt(a, b):
    return lax.dot_general(a, b, NT, preferred_element_type=F32)


def exact_dot(a, b):
    return lax.dot_general(
        a,
        b,
        (((1,), (0,)), ((), ())),
        preferred_element_type=F32,
        precision=lax.Precision.HIGHEST,
    )


def frequencies():
    frame = 10000.0 ** (-2.0 * np.arange(8) / 16)
    side = 10000.0 ** (-2.0 * np.arange(12) / 24)
    pairs = np.concatenate([frame, side, side])
    return np.tile(np.repeat(pairs, 2), 3)[None, :].astype(np.float32)


def kernel(
    hidden_far,
    modulation_far,
    positions_far,
    text_len_far,
    counts_row_far,
    counts_far,
    freq_far,
    latent_far,
    guidance_far,
    solver_far,
    out_mod_far,
    w_proj_far,
    w_qkv,
    w_out,
    w_up,
    w_down,
    out,
    hidden,
    modulation,
    positions,
    text_len,
    counts_row,
    counts,
    freq,
    latent,
    guidance,
    solver,
    out_mod,
    w_proj,
    wqkv,
    wout,
    wup,
    wdown,
    ag1a,
    ag1b,
    ag2a,
    ag2b,
    rows32,
    kv,
    rs1,
    rs2,
    swap,
    w_send,
    w_recv,
    near_sem,
    local_sem,
    c_send,
    c_recv,
    g_send,
    g_recv,
):
    cfg = lax.axis_index("cfg")
    me = lax.axis_index("seq")
    z, y, x = me // 16, (me // 4) % 4, me % 4

    def dev(axis, step):
        zz = (z + step) % 4 if axis == "z" else z
        yy = (y + step) % 4 if axis == "y" else y
        xx = (x + step) % 4 if axis == "x" else x
        return (cfg, zz * 16 + yy * 4 + xx)

    place = {"x": x, "y": y, "z": z}
    sibling = (1 - cfg, me)
    sends = []

    def remote(src, dst, send, recv, device):
        copy = pltpu.make_async_remote_copy(
            src_ref=src,
            dst_ref=dst,
            send_sem=send,
            recv_sem=recv,
            device_id=device,
            device_id_type=pl.DeviceIdType.MESH,
        )
        copy.start()
        sends.append(copy)
        return copy

    barrier = pltpu.get_barrier_semaphore()
    everyone = [dev(axis, step) for axis in "xyz" for step in (1, 2, 3)] + [sibling]
    for device in everyone:
        pl.semaphore_signal(
            barrier, inc=1, device_id=device, device_id_type=pl.DeviceIdType.MESH
        )

    near = []
    for i, (far, ref) in enumerate(
        (
            (hidden_far, hidden),
            (modulation_far, modulation),
            (positions_far, positions),
            (text_len_far, text_len),
            (counts_row_far, counts_row),
            (counts_far, counts),
            (freq_far, freq),
            (latent_far, latent),
            (guidance_far, guidance),
            (solver_far, solver),
            (out_mod_far, out_mod),
            (w_proj_far, w_proj),
        )
    ):
        copy = pltpu.make_async_copy(far, ref, near_sem.at[i])
        copy.start()
        near.append(copy)

    top, bottom = pl.ds(0, HID // 2), pl.ds(HID // 2, HID // 2)
    weights = {
        "k": (0, w_qkv.at[1], lambda i: wqkv.at[1, i], "x"),
        "v": (1, w_qkv.at[2], lambda i: wqkv.at[2, i], "x"),
        "q": (2, w_qkv.at[0], lambda i: wqkv.at[0, i], "x"),
        "out": (3, w_out, lambda i: wout.at[i], "x"),
        "up0": (4, w_up.at[top], lambda i: wup.at[i, top], "y"),
        "up1": (5, w_up.at[bottom], lambda i: wup.at[i, bottom], "y"),
        "down0": (6, w_down.at[top], lambda i: wdown.at[i, top], "y"),
        "down1": (7, w_down.at[bottom], lambda i: wdown.at[i, bottom], "y"),
    }
    start = pl.multiple_of(cfg * HALF, HALF)
    half = pl.ds(start, HALF)
    quarters = (
        pl.ds(start, HALF // 2),
        pl.ds(pl.multiple_of(start + HALF // 2, HALF // 2), HALF // 2),
    )
    turns = (1, 3)
    moving = {}
    local = []

    def send_weight(name):
        slot, src, dst, axis = weights[name]
        moving[name, 0] = [
            remote(
                src.at[:, half],
                dst(place[axis]).at[:, half],
                w_send.at[slot, 0, i],
                w_recv.at[slot, 0, i],
                dev(axis, turn),
            )
            for i, turn in enumerate(turns)
        ]

    def pass_weight(name):
        slot, src, dst, axis = weights[name]
        moving[name, 1], moving[name, 2] = [], []
        for i, turn in enumerate(turns):
            moving[name, 0][i].wait_recv()
            block = dst((place[axis] - turn + 4) % 4)
            moving[name, 1].append(
                remote(
                    block.at[:, quarters[i]],
                    block.at[:, quarters[i]],
                    w_send.at[slot, 1, i],
                    w_recv.at[slot, 1, i],
                    dev(axis, turn),
                )
            )
            moving[name, 2].append(
                remote(
                    block.at[:, half],
                    block.at[:, half],
                    w_send.at[slot, 2, i],
                    w_recv.at[slot, 2, i],
                    sibling,
                )
            )

    def end_weight(name):
        slot, src, dst, axis = weights[name]
        for copy in moving[name, 1]:
            copy.wait_recv()
        block = dst((place[axis] + 2) % 4)
        moving[name, 2].append(
            remote(
                block.at[:, half],
                block.at[:, half],
                w_send.at[slot, 3, 0],
                w_recv.at[slot, 3, 0],
                sibling,
            )
        )

    def have_weight(name):
        for copy in moving[name, 2]:
            copy.wait_recv()
        local[weights[name][0]].wait()

    for copy in near[:4]:
        copy.wait()
    resid = hidden[...].astype(F32)
    row = lax.broadcasted_iota(jnp.int32, (ROWS, 1), 0)
    is_text = me * ROWS + row < text_len[0]

    def modul(k):
        two = modulation[k]
        return jnp.where(is_text, two[0:1, :], two[1:2, :])

    normed = (layer_norm(resid, 1e-05) * (1.0 + modul(1)) + modul(0)).astype(BF)

    def gather_own(bufs, values, orders):
        for buf, value, (p, q) in zip(bufs, values, orders):
            for i, part in enumerate(value):
                lo = 0 if i == 0 else HALF
                buf[place[q], place[p], :, lo : lo + part.shape[1]] = part

    def gather_first(bufs, orders, slot):
        first = []
        for h, (buf, (p, q)) in enumerate(zip(bufs, orders)):
            ref = buf.at[place[q], place[p]]
            first.append(
                [
                    remote(
                        ref,
                        ref,
                        g_send.at[slot, h, 0, step - 1],
                        g_recv.at[slot, h, 0, step - 1],
                        dev(p, step),
                    )
                    for step in (2, 1, 3)
                ]
            )
        first = [[right, left, far] for far, right, left in first]
        return first, [gather_pass(bufs[h], orders[h], slot, h, 0) for h in range(2)]

    def gather_pass(buf, order, slot, h, behind):
        p, q = order
        ref = buf.at[place[q], (place[p] - behind + 4) % 4]
        return [
            remote(
                ref,
                ref,
                g_send.at[slot, h, behind + 1, step - 1],
                g_recv.at[slot, h, behind + 1, step - 1],
                dev(q, step),
            )
            for step in (2, 1, 3)
        ]

    def gather_second(bufs, orders, slot, state):
        first, second = state
        for i, behind in enumerate((1, 3, 2)):
            for h in range(2):
                first[h][i].wait_recv()
                second[h] += gather_pass(bufs[h], orders[h], slot, h, behind)

    def gather_end(bufs, orders, outer, state):
        for copy in state[1][0] + state[1][1]:
            copy.wait_recv()
        for h, (buf, (p, q)) in enumerate(zip(bufs, orders)):
            for i in range(SIDE):
                for j in range(SIDE):
                    at = (i * SIDE + j if q == outer else j * SIDE + i) * ROWS
                    rows32[at : at + ROWS, h * HALF : (h + 1) * HALF] = buf[
                        i, j, :, 0:HALF
                    ].astype(F32)

    lane = lax.broadcasted_iota(jnp.int32, (ROWS, PAD), 1)
    line = lax.broadcasted_iota(jnp.int32, (ROWS, PAD), 0)
    pos = jnp.zeros((ROWS, PAD), F32)
    for k in range(3):
        for r in range(ROWS):
            at = positions[k, r].astype(F32)
            pos = jnp.where((lane == k) & (line == r), at, pos)
    pos = jnp.where(is_text, 0.0, pos).astype(BF)
    order_one = (("y", "z"), ("y", "z"))
    bufs_one = (ag1a, ag1b)
    gather_own(
        bufs_one, ((normed[:, 0:HALF], pos), (normed[:, HALF:D],)), order_one
    )

    pl.semaphore_wait(barrier, len(everyone))

    state = gather_first(bufs_one, order_one, 0)
    for name in ("k", "v", "up0", "up1"):
        send_weight(name)
    for slot, src, dst, axis in weights.values():
        copy = pltpu.make_async_copy(src, dst(place[axis]), local_sem.at[slot])
        copy.start()
        local.append(copy)
    gather_second(bufs_one, order_one, 0, state)
    for copy in near[4:]:
        copy.wait()
    pass_weight("k")
    pass_weight("v")
    send_weight("q")
    send_weight("out")

    lane_a = lax.broadcasted_iota(jnp.int32, (HC, HC), 0)
    lane_b = lax.broadcasted_iota(jnp.int32, (HC, HC), 1)
    average = jnp.where(lane_a // HD == lane_b // HD, 1.0 / HD, 0.0).astype(F32)
    turn = (
        jnp.where((lane_a == lane_b + 1) & (lane_b % 2 == 0), -1.0, 0.0)
        + jnp.where((lane_a + 1 == lane_b) & (lane_b % 2 == 1), 1.0, 0.0)
    ).astype(F32)
    key = lax.broadcasted_iota(jnp.int32, (64, 512), 1)
    owner = (key // 32) % 4 * 16 + (key // 8) % 4 * 4 + key // 128
    pick = jnp.where(lax.broadcasted_iota(jnp.int32, (64, 512), 0) == owner, 1.0, 0.0)
    count_of = exact_dot(
        jnp.broadcast_to(counts_row[...].astype(F32), (ROWS, 64)), pick.astype(F32)
    )
    key_row = lax.broadcasted_iota(jnp.int32, (ROWS, 512), 1) % ROWS
    live = jnp.where(key_row.astype(F32) < count_of, 1.0, 0.0)[0:1, :]
    dim = lax.broadcasted_iota(jnp.int32, (PAD, HC), 1) % HD
    which = jnp.where(dim < 16, 0, jnp.where(dim < 40, 1, 2))
    axis_of = jnp.where(
        lax.broadcasted_iota(jnp.int32, (PAD, HC), 0) == which, 1.0, 0.0
    ).astype(F32)

    end_weight("k")
    end_weight("v")
    pass_weight("up0")
    send_weight("down0")
    gather_end(bufs_one, order_one, "z", state)
    for z_at in range(SIDE):
        for y_at in range(SIDE):
            at = (z_at * SIDE + y_at) * ROWS
            swap[at : at + ROWS, :] = ag1a[z_at, y_at, :, HALF : HALF + PAD].astype(F32)
    angles = exact_dot(swap[...], axis_of) * freq[...]
    cosine = jnp.cos(angles)
    sine = jnp.sin(angles)
    tokens = rows32[...].astype(BF)

    def heads(columns):
        values = columns.astype(BF).astype(F32)
        center = values - exact_dot(values, average)
        spread = exact_dot(center * center, average)
        unit = center * lax.rsqrt(spread + 1e-06)
        return unit * cosine + exact_dot(unit, turn) * sine

    def project(part):
        return dot_nt(tokens, wqkv[part].reshape(HC, D))

    pass_weight("q")
    have_weight("k")
    keys = heads(project(1)).astype(BF)
    have_weight("v")
    kv[x, :, 0:HC] = keys
    kv[x, :, HC : 2 * HC] = project(2).astype(BF)
    moved = [
        remote(
            kv.at[x],
            kv.at[x],
            c_send.at[4, 0, 0, step - 1],
            c_recv.at[4, 0, 0, step - 1],
            dev("x", step),
        )
        for step in (2, 1, 3)
    ]
    end_weight("q")
    pass_weight("out")
    pass_weight("up1")
    have_weight("q")
    queries = (heads(project(0)) * HD ** (-0.5)).astype(BF)
    for copy in moved:
        copy.wait_recv()
    end_weight("out")

    all_keys = kv[:, :, 0:HC].reshape(4 * 128, HC)
    all_values = kv[:, :, 128 : 2 * HC].reshape(4 * 128, 2 * HC - 128)
    lane_q = lax.broadcasted_iota(jnp.int32, (1, HC), 1) // HD
    lane_v = lax.broadcasted_iota(jnp.int32, (1, 256), 1) // HD - 1
    context = jnp.zeros((128, 256), F32)
    for head in range(HC // HD):
        chosen = jnp.where(lane_q == head, queries, jnp.zeros_like(queries))
        attend = jnp.exp(dot_nt(chosen, all_keys)) * live
        denom = jnp.sum(attend, axis=1, keepdims=True)
        numer = jnp.dot(attend.astype(BF), all_values, preferred_element_type=F32)
        context = jnp.where(lane_v == head, numer / denom, context)
    context = context[:, 64:256].astype(BF)
    have_weight("out")

    def scatter_sum(send, recv, mid, last, produce, p, q, slot, hooks):
        order = ((q, p), (p, q))
        copies = [[], []]
        for h in range(2):
            part = produce(h)
            for q_at in range(SIDE):
                for p_at in range(SIDE):
                    at = (q_at * SIDE + p_at) * ROWS
                    i, j = (q_at, p_at) if h == 0 else (p_at, q_at)
                    send[h, i, j] = part[at : at + ROWS, :].astype(BF)
            for step in (2, 1, 3):
                one = order[h][0]
                copies[h].append(
                    remote(
                        send.at[h, (place[one] + step) % 4],
                        recv.at[h, step - 1],
                        c_send.at[slot, 0, h, step - 1],
                        c_recv.at[slot, 0, h, step - 1],
                        dev(one, step),
                    )
                )
        hooks[0]()
        second = [[], []]
        for h in range(2):
            one, two = order[h]
            for copy in copies[h]:
                copy.wait_recv()
            for j in range(SIDE):
                total = send[h, place[one], j].astype(F32)
                for k in range(3):
                    total = total + recv[h, k, j].astype(F32)
                mid[h, j] = total.astype(BF)
            for step in (2, 1, 3):
                second[h].append(
                    remote(
                        mid.at[h, (place[two] + step) % 4],
                        last.at[h, step - 1],
                        c_send.at[slot, 1, h, step - 1],
                        c_recv.at[slot, 1, h, step - 1],
                        dev(two, step),
                    )
                )
        hooks[1]()
        halves = []
        for h in range(2):
            one, two = order[h]
            for copy in second[h]:
                copy.wait_recv()
            total = mid[h, place[two]].astype(F32)
            for k in range(3):
                total = total + last[h, k].astype(F32)
            halves.append(total)
        return jnp.concatenate(halves, axis=1)

    out_weight = wout[...].reshape(HC, D)
    attended = scatter_sum(
        *rs1,
        lambda h: jnp.dot(
            context, out_weight[:, h * HALF : (h + 1) * HALF], preferred_element_type=F32
        ),
        "y",
        "z",
        1,
        (lambda: pass_weight("down0"), lambda: send_weight("down1")),
    )
    first_res = resid + modul(2) * attended
    normed_two = (layer_norm(first_res, 1e-05) * (1.0 + modul(4)) + modul(3)).astype(BF)
    order_two = (("x", "z"), ("z", "x"))
    bufs_two = (ag2a, ag2b)
    gather_own(
        bufs_two, ((normed_two[:, 0:HALF],), (normed_two[:, HALF:D],)), order_two
    )
    state = gather_first(bufs_two, order_two, 1)
    gather_second(bufs_two, order_two, 1, state)
    end_weight("up0")
    end_weight("up1")
    end_weight("down0")
    pass_weight("down1")
    gather_end(bufs_two, order_two, "z", state)
    tokens_two = rows32[...].astype(BF)
    have_weight("up0")
    have_weight("up1")
    inner = jax.nn.gelu(
        dot_nt(tokens_two, wup[...].reshape(SIDE * HID, D)), approximate=True
    ).astype(BF)
    end_weight("down1")
    have_weight("down0")
    have_weight("down1")
    down_weight = wdown[...].reshape(SIDE * HID, D)
    reduced = scatter_sum(
        *rs2,
        lambda h: jnp.dot(
            inner, down_weight[:, h * HALF : (h + 1) * HALF], preferred_element_type=F32
        ),
        "x",
        "z",
        3,
        (lambda: None, lambda: None),
    )
    second_res = first_res + modul(5) * reduced
    final = (
        layer_norm(second_res, 1e-05) * (1.0 + out_mod[1:2, :]) + out_mod[0:1, :]
    ).astype(BF)
    prediction = dot_nt(final, w_proj[...])
    swap[0:ROWS, 0:64] = prediction
    other = remote(
        swap.at[0:ROWS], swap.at[ROWS : 2 * ROWS], c_send.at[4, 1, 0, 0], c_recv.at[4, 1, 0, 0], sibling
    )
    other.wait_recv()
    theirs = swap[ROWS : 2 * ROWS, 0:64]
    is_cond = cfg == 0
    pred_cond = jnp.where(is_cond, prediction, theirs)
    pred_uncond = jnp.where(is_cond, theirs, prediction)
    guided = pred_uncond + guidance[0] * (pred_cond - pred_uncond)
    guided = jnp.where(is_cond, guided[:, 0:32], guided[:, 32:64])
    updated = solver[0] * latent[...] + solver[1] * guided
    keep = (row < counts[me]) & jnp.logical_not(is_text)
    out[...] = jnp.where(keep, updated, latent[...])
    for copy in sends:
        copy.wait_send()


def shards(
    hidden,
    latent,
    positions,
    counts,
    text_len,
    modulation,
    w_qkv,
    w_out,
    w_up,
    w_down,
    out_mod,
    w_proj,
    guidance,
    solver,
):
    vmem = pl.BlockSpec(memory_space=pltpu.VMEM)
    whole = pl.BlockSpec(memory_space=pl.ANY)

    def sums():
        return (
            pltpu.VMEM((2, SIDE, SIDE, ROWS, HALF), BF),
            pltpu.VMEM((2, 3, SIDE, ROWS, HALF), BF),
            pltpu.VMEM((2, SIDE, ROWS, HALF), BF),
            pltpu.VMEM((2, 3, ROWS, HALF), BF),
        )

    return pl.pallas_call(
        kernel,
        out_shape=jax.ShapeDtypeStruct(latent.shape, F32),
        in_specs=[whole] * 16,
        out_specs=vmem,
        scratch_shapes=[
            pltpu.VMEM((ROWS, D), BF),
            pltpu.VMEM((6, 2, D), F32),
            pltpu.SMEM((3, ROWS), jnp.int32),
            pltpu.SMEM((1,), jnp.int32),
            pltpu.VMEM((1, 64), jnp.int32),
            pltpu.SMEM((64,), jnp.int32),
            pltpu.VMEM((1, HC), F32),
            pltpu.VMEM((ROWS, 32), F32),
            pltpu.SMEM((1,), F32),
            pltpu.SMEM((2,), F32),
            pltpu.VMEM((2, D), F32),
            pltpu.VMEM((64, D), BF),
            pltpu.VMEM((3, SIDE, 48, D), BF),
            pltpu.VMEM((SIDE, 48, D), BF),
            pltpu.VMEM((SIDE, HID, D), BF),
            pltpu.VMEM((SIDE, HID, D), BF),
            pltpu.VMEM((SIDE, SIDE, ROWS, HALF + PAD), BF),
            pltpu.VMEM((SIDE, SIDE, ROWS, HALF), BF),
            pltpu.VMEM((SIDE, SIDE, ROWS, HALF), BF),
            pltpu.VMEM((SIDE, SIDE, ROWS, HALF), BF),
            pltpu.VMEM((SIDE * SIDE * ROWS, D), F32),
            pltpu.VMEM((SIDE, SIDE * SIDE * ROWS, 2 * HC), BF),
            sums(),
            sums(),
            pltpu.VMEM((SIDE * SIDE * ROWS, PAD), F32),
            pltpu.SemaphoreType.DMA((8, 4, 2)),
            pltpu.SemaphoreType.DMA((8, 4, 2)),
            pltpu.SemaphoreType.DMA((12,)),
            pltpu.SemaphoreType.DMA((8,)),
            pltpu.SemaphoreType.DMA((5, 2, 2, 3)),
            pltpu.SemaphoreType.DMA((5, 2, 2, 3)),
            pltpu.SemaphoreType.DMA((2, 2, 5, 3)),
            pltpu.SemaphoreType.DMA((2, 2, 5, 3)),
        ],
        compiler_params=pltpu.CompilerParams(
            collective_id=0, has_side_effects=True, vmem_limit_bytes=56 << 20
        ),
        name="step",
    )(
        hidden[0],
        modulation.transpose(1, 0, 2),
        positions.T,
        text_len,
        counts[None, :],
        counts,
        jnp.asarray(frequencies()),
        latent,
        guidance,
        solver,
        out_mod,
        w_proj.T,
        w_qkv.transpose(1, 2, 0),
        w_out,
        w_up.T,
        w_down,
    )


def solution(mesh):
    in_specs = (
        P("cfg", "seq", None),
        P("seq", "cfg"),
        P("seq", None),
        P(),
        P(),
        P(),
        P(None, None, "seq"),
        P("seq", None),
        P(None, "seq"),
        P("seq", None),
        P(),
        P(),
        P(),
        P(),
    )
    return jax.shard_map(
        shards, mesh=mesh, in_specs=in_specs, out_specs=P("seq", "cfg"), check_vma=False
    )
```
